32 devices in a mesh: dp: 8 (over z, x), tensor: 4 (over y, core).
Axes of the slice: x: 2, y: 2, z: 4, core: 2. Of those that a mesh axis runs over, the one named last changes fastest.
Arguments:
- inputs: bfloat16 [2048, 2048], P('dp'), may hold values from -6 to 6
- document: int32 [2048], P('dp'), may hold values from 0 to 8, as said below
- query_weight: bfloat16 [2048, 2048], P(None, 'tensor'), may hold values from -0.125 to 0.125
- key_weight: bfloat16 [2048, 2048], P(None, 'tensor'), may hold values from -0.125 to 0.125
- value_weight: bfloat16 [2048, 3456], P(None, 'tensor'), may hold values from -0.125 to 0.125
- gate_weight: bfloat16 [2048, 3456], P(None, 'tensor'), may hold values from -0.125 to 0.125
- out_weight: bfloat16 [3456, 2048], P('tensor'), may hold values from -0.109375 to 0.109375
- inner_weight: bfloat16 [2048, 3456], P(None, 'tensor'), may hold values from -0.125 to 0.125
- linear_weight: bfloat16 [2048, 3456], P(None, 'tensor'), may hold values from -0.125 to 0.125
- down_weight: bfloat16 [3456, 2048], P('tensor'), may hold values from -0.109375 to 0.109375
- first_gain: float32 [2048], replicated, may hold values from 0.5 to 1.5
- first_bias: float32 [2048], replicated, may hold values from -3 to 3
- head_gain: float32 [3456], P('tensor'), may hold values from 0.5 to 1.5
- second_gain: float32 [2048], replicated, may hold values from 0.5 to 1.5
- second_bias: float32 [2048], replicated, may hold values from -3 to 3
- cotangent: bfloat16 [2048, 2048], P('dp'), may hold values from -8 to 8
Outputs:
- outputs: float32 [2048, 2048], P('dp')
- grad_inputs: float32 [2048, 2048], P('dp')
- grad_query: float32 [2048, 2048], P('dp', 'tensor')
- grad_key: float32 [2048, 2048], P('dp', 'tensor')
- grad_value: float32 [2048, 3456], P('dp', 'tensor')
- grad_gate: float32 [2048, 3456], P('dp', 'tensor')
- grad_out: float32 [3456, 2048], P('tensor', 'dp')
- grad_inner: float32 [2048, 3456], P('dp', 'tensor')
- grad_linear: float32 [2048, 3456], P('dp', 'tensor')
- grad_down: float32 [3456, 2048], P('tensor', 'dp')
- grad_first_gain: float32 [2048], replicated
- grad_first_bias: float32 [2048], replicated
- grad_head_gain: float32 [3456], P('tensor')
- grad_second_gain: float32 [2048], replicated
- grad_second_bias: float32 [2048], replicated
The draws below stay inside these ranges and needn't reach their ends.
Inputs may be any that keep to these rules, and one draw needn't show every extreme that they name: `document`: within each dp block of 256 slots the sequence numbers never fall; the live slots come first and hold numbers below 8, the last live one 8 - 1; the other slots hold 8. One block is all live and another has exactly 128 live slots.
All inputs are finite; a program needn't handle non-finite values.
Results may differ from the reference program's by a relative error of at most 0.015.
Values sent between devices are 32-bit elements; how exact they have to be, the bound alone decides.
No kernel may reach another device: no remote copies, remote signals or barrier semaphores. Data moves between devices by JAX's collectives and lax.ppermute only.
A program may use at most 192 MiB of HBM per device.

```python
import jax
import jax.numpy as jnp
from jax import lax

D = 2048
HEADS = 8
KD = 256
VD = 432
FF = 3456
TOK_DEV = 256
DOCS_DEV = 8
QK = 2048
V = 3456
TOKENS = 2048


def draw_document(key, part):
    blocks = TOKENS // TOK_DEV
    key_live, key_full, key_short, key_cuts = jax.random.split(key, 4)
    live = jax.random.randint(key_live, (blocks,), TOK_DEV // 2, TOK_DEV + 1)
    full_block = jax.random.randint(key_full, (), 0, blocks)
    short_block = (full_block + 1 + jax.random.randint(key_short, (), 0, blocks - 1)) % blocks
    indices = jnp.arange(blocks)
    live = jnp.where(indices == full_block, TOK_DEV, jnp.where(indices == short_block, TOK_DEV // 2, live))
    raw_cuts = jax.random.randint(key_cuts, (blocks, DOCS_DEV - 1), 0, 1048576)
    cuts = raw_cuts % (live[:, None] - 1) + 1
    places = jnp.arange(TOK_DEV)
    docs = jnp.sum((places[None, :, None] >= cuts[:, None, :]).astype(jnp.int32), axis=2)
    docs = jnp.where(places[None, :] < live[:, None], docs, DOCS_DEV)
    return docs.reshape(TOKENS).astype(jnp.int32)


def spiked(values, rng, source, target, shards_of, factor):
    owner, partner = [(jnp.arange(values.shape[position]) // (values.shape[position] // shards_of)).reshape([-1 if axis == position else 1 for axis in range(values.ndim)]) for position in (source, target)]
    chosen = jax.random.permutation(rng, shards_of)[partner]
    strong = (owner == chosen) | (owner == (partner + shards_of // 2) % shards_of)
    return jnp.where(strong, factor * values, values)


def steps_of(key, shape, shards, least, top_value):
    loudness = 1.0
    for axis_at, shards_of in shards:
        draws = jax.random.uniform(jax.random.fold_in(jax.random.fold_in(key, 6), axis_at), (shards_of,), jnp.float32, least / len(shards), top_value / len(shards))
        loudness = loudness * jnp.repeat(jnp.exp(draws), shape[axis_at] // shards_of).reshape((-1,) + (1,) * (len(shape) - 1 - axis_at))
    return loudness


def normal_values(rng, dims, scale, most, cuts=(), held_as=jnp.bfloat16):
    loudness = steps_of(rng, dims, cuts, -0.22, 0.18) if cuts else 1.0
    drawn = jax.random.normal(rng, dims, jnp.float32) * scale * loudness
    return jnp.minimum(jnp.maximum(drawn, -most), most).astype(held_as)


def gaussian_with(key, shape, scale, limit, cuts, heavy, dtype=jnp.bfloat16):
    drawn = scale * jax.random.normal(key, shape, jnp.float32)
    if cuts:
        drawn = drawn * steps_of(key, shape, cuts, -0.22, 0.18)
    return jnp.clip(spiked(drawn, jax.random.fold_in(key, 3), *heavy), -limit, limit).astype(dtype)


def setup_inputs(seed: int = 0) -> dict:
    streams_of = jax.random.split(jax.random.key(seed), 17)
    inputs = normal_values(streams_of[0], (TOKENS, D), 1.0, 6.0, ((0, 8),))
    document = draw_document(jax.random.fold_in(streams_of[16], 71), 0)
    query_weight = normal_values(streams_of[2], (D, QK), D ** -0.5, 0.125, ((1, 4),))
    key_weight = normal_values(streams_of[3], (D, QK), D ** -0.5, 0.125, ((1, 4),))
    value_weight = normal_values(streams_of[4], (D, V), D ** -0.5, 0.125, ((1, 4),))
    gate_weight = normal_values(streams_of[5], (D, V), D ** -0.5, 0.125, ((1, 4),))
    out_weight = normal_values(streams_of[6], (V, D), V ** -0.5, 0.109375, ((0, 4),))
    inner_weight = normal_values(streams_of[7], (D, FF), D ** -0.5, 0.125, ((1, 4),))
    linear_weight = normal_values(streams_of[8], (D, FF), D ** -0.5, 0.125, ((1, 4),))
    down_weight = normal_values(streams_of[9], (FF, D), FF ** -0.5, 0.109375, ((0, 4),))
    first_gain = jnp.clip(1.0 + 0.1 * jax.random.normal(streams_of[10], (D,), jnp.float32), 0.5, 1.5)
    first_bias = normal_values(streams_of[11], (D,), 0.5, 3.0, (), jnp.float32)
    head_gain = jnp.clip(1.0 + 0.1 * jax.random.normal(streams_of[12], (V,), jnp.float32), 0.5, 1.5)
    second_gain = jnp.clip(1.0 + 0.1 * jax.random.normal(streams_of[13], (D,), jnp.float32), 0.5, 1.5)
    second_bias = normal_values(streams_of[14], (D,), 0.5, 3.0, (), jnp.float32)
    cotangent = gaussian_with(streams_of[15], (TOKENS, D), 1.0, 8.0, ((0, 8),), (0, 1, 8, 2.0))
    return {"inputs": inputs, "document": document, "query_weight": query_weight, "key_weight": key_weight, "value_weight": value_weight, "gate_weight": gate_weight, "out_weight": out_weight, "inner_weight": inner_weight, "linear_weight": linear_weight, "down_weight": down_weight, "first_gain": first_gain, "first_bias": first_bias, "head_gain": head_gain, "second_gain": second_gain, "second_bias": second_bias, "cotangent": cotangent}


EPS = 1e-05
HEAD_EPS = 0.25

def norm_rows(value, gain, bias, epsilon):
    center = value - lax.optimization_barrier(jnp.mean(value, -1, keepdims=True))
    inverse = lax.rsqrt(lax.optimization_barrier(jnp.mean(center * center, -1, keepdims=True)) + epsilon)
    unit = center * inverse
    return (unit * gain + bias, unit, inverse)

def norm_back(upstream, unit, inverse, gain):
    scaled = upstream * gain
    result = inverse * (scaled - lax.optimization_barrier(jnp.mean(scaled, -1, keepdims=True)) - unit * lax.optimization_barrier(jnp.mean(scaled * unit, -1, keepdims=True)))
    return (result, lax.optimization_barrier(jnp.sum(upstream * unit, 0)), lax.optimization_barrier(jnp.sum(upstream, 0)))

def decay_table(document, first_head, head_count):
    heads = (first_head + jnp.arange(head_count)).astype(jnp.float32)
    log_rate = jnp.log1p(-jnp.exp2(-5.0 - heads))
    places = jnp.arange(document.shape[0])
    spread = (places[:, None] - places[None, :]).astype(jnp.float32)
    allowed = (places[:, None] >= places[None, :]) & (document[:, None] == document[None, :])
    safe = jnp.where(allowed, spread, 0.0)
    return jnp.where(allowed[None], jnp.exp(safe[None] * log_rate[:, None, None]), 0.0)

def one_block(inputs_bf, document, cotangent_bf, query_weight, key_weight, value_weight, gate_weight, out_weight, inner_weight, linear_weight, down_weight, first_gain, first_bias, head_gain, second_gain, second_bias):
    f32 = jnp.float32
    bf16 = jnp.bfloat16
    inputs = inputs_bf.astype(f32)
    cotangent = cotangent_bf.astype(f32)
    rows = inputs.shape[0]
    first_norm, first_hat, first_inv = norm_rows(inputs, first_gain, first_bias, EPS)
    normed_one = first_norm.astype(bf16)
    queries = jnp.dot(normed_one, query_weight, preferred_element_type=f32)
    keys_raw = jnp.dot(normed_one, key_weight, preferred_element_type=f32)
    values_raw = jnp.dot(normed_one, value_weight, preferred_element_type=f32)
    gates_raw = jnp.dot(normed_one, gate_weight, preferred_element_type=f32)
    query_bf = queries.astype(bf16).reshape(rows, HEADS, KD)
    key_bf = (keys_raw * KD ** (-0.5)).astype(bf16).reshape(rows, HEADS, KD)
    value_bf = values_raw.astype(bf16).reshape(rows, HEADS, VD)
    decay = decay_table(document, 0, HEADS)
    scores = jnp.einsum('nhk,mhk->hnm', query_bf.astype(f32), key_bf.astype(f32)) * decay
    score_bf = scores.astype(bf16)
    mixed = jnp.einsum('hnm,mhv->nhv', score_bf.astype(f32), value_bf.astype(f32))
    gain_heads = head_gain.reshape(HEADS, VD)
    normed_heads, head_hat, head_inv = norm_rows(mixed, gain_heads, 0.0, HEAD_EPS)
    normed_flat = normed_heads.reshape(rows, V)
    sigma = jax.nn.sigmoid(gates_raw)
    swish = gates_raw * sigma
    gated = (swish * normed_flat).astype(bf16)
    middle = inputs + jnp.dot(gated, out_weight, preferred_element_type=f32)
    second_norm, second_hat, second_inv = norm_rows(middle, second_gain, second_bias, EPS)
    normed_two = second_norm.astype(bf16)
    inner = jnp.dot(normed_two, inner_weight, preferred_element_type=f32)
    linear = jnp.dot(normed_two, linear_weight, preferred_element_type=f32)
    cumulative = 0.5 * (1.0 + jax.scipy.special.erf(inner * 0.7071067811865476))
    gelu_inner = inner * cumulative
    hidden = (gelu_inner * linear).astype(bf16)
    outputs = middle + jnp.dot(hidden, down_weight, preferred_element_type=f32)
    live = (document < DOCS_DEV).astype(f32)
    grad_top = cotangent * live[:, None]
    grad_top_bf = grad_top.astype(bf16)
    grad_down = jnp.dot(hidden.T, grad_top_bf, preferred_element_type=f32)
    grad_hidden = jnp.dot(grad_top_bf, down_weight.T, preferred_element_type=f32)
    slope = cumulative + inner * jnp.exp(-0.5 * inner * inner) * 0.3989422804014327
    grad_inner_bf = (grad_hidden * linear * slope).astype(bf16)
    grad_linear_bf = (grad_hidden * gelu_inner).astype(bf16)
    grad_inner = jnp.dot(normed_two.T, grad_inner_bf, preferred_element_type=f32)
    grad_linear = jnp.dot(normed_two.T, grad_linear_bf, preferred_element_type=f32)
    grad_normed_two = jnp.dot(grad_inner_bf, inner_weight.T, preferred_element_type=f32) + jnp.dot(grad_linear_bf, linear_weight.T, preferred_element_type=f32)
    part_two, grad_second_gain, grad_second_bias = norm_back(grad_normed_two, second_hat, second_inv, second_gain)
    grad_middle = grad_top + part_two
    grad_middle_bf = grad_middle.astype(bf16)
    grad_out = jnp.dot(gated.T, grad_middle_bf, preferred_element_type=f32)
    grad_gated = jnp.dot(grad_middle_bf, out_weight.T, preferred_element_type=f32)
    grad_gates_bf = (grad_gated * normed_flat * sigma * (1.0 + gates_raw * (1.0 - sigma))).astype(bf16)
    grad_normed = (grad_gated * swish).reshape(rows, HEADS, VD)
    grad_mixed, grad_gain_heads, unused_bias = norm_back(grad_normed, head_hat, head_inv, gain_heads)
    grad_mixed_bf = grad_mixed.astype(bf16)
    grad_scores = jnp.einsum('nhv,mhv->hnm', grad_mixed_bf.astype(f32), value_bf.astype(f32))
    grad_values = jnp.einsum('hnm,nhv->mhv', score_bf.astype(f32), grad_mixed_bf.astype(f32))
    grad_masked = (grad_scores * decay).astype(bf16)
    grad_queries = jnp.einsum('hnm,mhk->nhk', grad_masked.astype(f32), key_bf.astype(f32))
    grad_keys = jnp.einsum('hnm,nhk->mhk', grad_masked.astype(f32), query_bf.astype(f32)) * KD ** (-0.5)
    grad_queries_bf = grad_queries.astype(bf16).reshape(rows, QK)
    grad_keys_bf = grad_keys.astype(bf16).reshape(rows, QK)
    grad_values_bf = grad_values.astype(bf16).reshape(rows, V)
    grad_query = jnp.dot(normed_one.T, grad_queries_bf, preferred_element_type=f32)
    grad_key = jnp.dot(normed_one.T, grad_keys_bf, preferred_element_type=f32)
    grad_value = jnp.dot(normed_one.T, grad_values_bf, preferred_element_type=f32)
    grad_gate = jnp.dot(normed_one.T, grad_gates_bf, preferred_element_type=f32)
    grad_normed_one = jnp.dot(grad_queries_bf, query_weight.T, preferred_element_type=f32) + jnp.dot(grad_keys_bf, key_weight.T, preferred_element_type=f32) + jnp.dot(grad_values_bf, value_weight.T, preferred_element_type=f32) + jnp.dot(grad_gates_bf, gate_weight.T, preferred_element_type=f32)
    part_one, grad_first_gain, grad_first_bias = norm_back(grad_normed_one, first_hat, first_inv, first_gain)
    grad_inputs = grad_middle + part_one
    grads = (grad_query, grad_key, grad_value, grad_gate, grad_out, grad_inner, grad_linear, grad_down, grad_first_gain, grad_first_bias, grad_gain_heads.reshape(V), grad_second_gain, grad_second_bias)
    return (outputs, grad_inputs, grads)

def reference(inputs, document, query_weight, key_weight, value_weight, gate_weight, out_weight, inner_weight, linear_weight, down_weight, first_gain, first_bias, head_gain, second_gain, second_bias, cotangent):
    blocks = TOKENS // TOK_DEV
    weights = (query_weight, key_weight, value_weight, gate_weight, out_weight, inner_weight, linear_weight, down_weight, first_gain, first_bias, head_gain, second_gain, second_bias)
    zeros = (jnp.zeros((D, QK), jnp.float32), jnp.zeros((D, QK), jnp.float32), jnp.zeros((D, V), jnp.float32), jnp.zeros((D, V), jnp.float32), jnp.zeros((V, D), jnp.float32), jnp.zeros((D, FF), jnp.float32), jnp.zeros((D, FF), jnp.float32), jnp.zeros((FF, D), jnp.float32), jnp.zeros((D,), jnp.float32), jnp.zeros((D,), jnp.float32), jnp.zeros((V,), jnp.float32), jnp.zeros((D,), jnp.float32), jnp.zeros((D,), jnp.float32))

    def step(carry, pieces):
        block_in, block_doc, block_ct = pieces
        outputs, grad_inputs, grads = one_block(block_in, block_doc, block_ct, *weights)
        return (tuple((total + piece for total, piece in zip(carry, grads))), (outputs, grad_inputs))
    totals, stacked = lax.scan(step, zeros, (inputs.reshape(blocks, TOK_DEV, D), document.reshape(blocks, TOK_DEV), cotangent.reshape(blocks, TOK_DEV, D)))
    outputs = stacked[0].reshape(TOKENS, D)
    grad_inputs = stacked[1].reshape(TOKENS, D)
    return (outputs, grad_inputs, totals[0], totals[1], totals[2], totals[3], totals[4], totals[5], totals[6], totals[7], totals[8], totals[9], totals[10], totals[11], totals[12])
```

```python
import jax
import jax.numpy as jnp
from jax import lax
from jax.sharding import PartitionSpec as P

KD = 256
VD = 432
DOCS_DEV = 8
GROUP = 4
PAIR = 2

EPS = 1e-05
HEAD_EPS = 0.25

F32 = jnp.float32
BF16 = jnp.bfloat16
AXES = ("dp", "tensor")


def dot(a, b, contract):
    return lax.dot_general(a, b, (contract, ((), ())), preferred_element_type=F32)


def nn(a, b):
    return dot(a, b, ((1,), (0,)))


def nt(a, b):
    return dot(a, b, ((1,), (1,)))


def tn(a, b):
    return dot(a, b, ((0,), (0,)))


def bdot(a, b, ca, cb):
    return lax.dot_general(a, b, (((ca,), (cb,)), ((0,), (0,))), preferred_element_type=F32)


def norm_rows(value, gain, bias, epsilon):
    center = value - jnp.mean(value, -1, keepdims=True)
    inverse = lax.rsqrt(jnp.mean(center * center, -1, keepdims=True) + epsilon)
    unit = center * inverse
    return (unit * gain + bias, unit, inverse)


def norm_back(upstream, unit, inverse, gain):
    scaled = upstream * gain
    return inverse * (
        scaled
        - jnp.mean(scaled, -1, keepdims=True)
        - unit * jnp.mean(scaled * unit, -1, keepdims=True)
    )


def decay_tables(document, first_head, head_count):
    rows = document.shape[1]
    places = jnp.arange(rows)
    spread = (places[:, None] - places[None, :]).astype(F32)
    allowed = (places[:, None] >= places[None, :])[None] & (
        document[:, :, None] == document[:, None, :]
    )
    safe = jnp.where(allowed, spread[None], 0.0)
    tables = []
    for h in range(head_count):
        log_rate = jnp.log1p(-jnp.exp2(-5.0 - (first_head + h).astype(F32)))
        tables.append(jnp.where(allowed, jnp.exp(safe * log_rate), 0.0))
    return tables


def head_mean(value, head_count):
    column = lax.broadcasted_iota(jnp.int32, (1, value.shape[1]), 1)
    out = None
    for h in range(head_count):
        mine = (column >= h * VD) & (column < (h + 1) * VD)
        mean = jnp.sum(jnp.where(mine, value, 0.0), -1, keepdims=True) * (1.0 / VD)
        out = mean if out is None else jnp.where(column >= h * VD, mean, out)
    return out


def by_head(parts):
    column = lax.broadcasted_iota(jnp.int32, (1, 1, parts[0].shape[-1]), 2)
    out = parts[0]
    for h in range(1, len(parts)):
        out = jnp.where(column >= h * VD, parts[h], out)
    return out


def head_only(value, h):
    column = lax.broadcasted_iota(jnp.int32, (1, value.shape[1]), 1)
    mine = (column >= h * VD) & (column < (h + 1) * VD)
    return jnp.where(mine, value, jnp.zeros((), value.dtype))


def retention_forward(normed, document, weights, head_gain, first_head):
    query_weight, key_weight, value_weight, gate_weight = weights
    blocks, rows = document.shape
    heads = query_weight.shape[1] // KD
    query = nn(normed, query_weight).astype(BF16)
    key = (nn(normed, key_weight) * KD ** (-0.5)).astype(BF16)
    value = nn(normed, value_weight).astype(BF16)
    gates = nn(normed, gate_weight)
    decay = decay_tables(document, first_head, heads)
    cube = lambda z: z.reshape(blocks, rows, z.shape[-1])
    value3 = cube(value)
    scores, parts, queries, keys = [], [], [], []
    for h in range(heads):
        queries.append(cube(query[:, h * KD : (h + 1) * KD]))
        keys.append(cube(key[:, h * KD : (h + 1) * KD]))
        scores.append((bdot(queries[h], keys[h], 2, 2) * decay[h]).astype(BF16))
        parts.append(bdot(scores[h], value3, 2, 1))
    mixed = by_head(parts).reshape(blocks * rows, value.shape[1])
    center = mixed - head_mean(mixed, heads)
    inverse = lax.rsqrt(head_mean(center * center, heads) + HEAD_EPS)
    hat = center * inverse
    normed_heads = hat * head_gain
    sigma = jax.nn.sigmoid(gates)
    swish = gates * sigma
    gated = (swish * normed_heads).astype(BF16)
    return gated, (queries, keys, value3, scores, decay, gates, hat, inverse)


def retention_backward(grad_middle_bf, state, out_weight, head_gain):
    queries, keys, value3, scores, decay, gates, hat, inverse = state
    heads = len(scores)
    blocks, rows, width = value3.shape
    grad_gated = nt(grad_middle_bf, out_weight)
    sigma = jax.nn.sigmoid(gates)
    swish = gates * sigma
    normed_heads = hat * head_gain
    grad_gates = (grad_gated * normed_heads * sigma * (1.0 + gates * (1.0 - sigma))).astype(BF16)
    grad_normed = grad_gated * swish
    scaled = grad_normed * head_gain
    grad_mixed = (
        inverse * (scaled - head_mean(scaled, heads) - hat * head_mean(scaled * hat, heads))
    ).astype(BF16)
    cube = lambda z: z.reshape(blocks, rows, z.shape[-1])
    flat = lambda z: z.reshape(blocks * rows, z.shape[-1])
    mixed3 = cube(grad_mixed)
    grad_query, grad_key, parts = [], [], []
    for h in range(heads):
        grad_scores = bdot(cube(head_only(grad_mixed, h)), value3, 2, 2)
        masked = (grad_scores * decay[h]).astype(BF16)
        grad_query.append(flat(bdot(masked, keys[h], 2, 1).astype(BF16)))
        grad_key.append(flat((bdot(masked, queries[h], 1, 1) * KD ** (-0.5)).astype(BF16)))
        parts.append(bdot(scores[h], mixed3, 1, 1))
    grad_value = flat(by_head(parts).astype(BF16))
    return (
        jnp.concatenate(grad_query, 1),
        jnp.concatenate(grad_key, 1),
        grad_value,
        grad_gates,
        grad_normed,
    )


def mlp(normed, grad_top_bf, inner_weight, linear_weight, down_weight):
    inner = nn(normed, inner_weight)
    linear = nn(normed, linear_weight)
    grad_hidden = nt(grad_top_bf, down_weight)
    cumulative = 0.5 * (1.0 + jax.scipy.special.erf(inner * 0.7071067811865476))
    gelu_inner = inner * cumulative
    hidden = (gelu_inner * linear).astype(BF16)
    slope = cumulative + inner * jnp.exp(-0.5 * inner * inner) * 0.3989422804014327
    grad_inner = (grad_hidden * linear * slope).astype(BF16)
    grad_linear = (grad_hidden * gelu_inner).astype(BF16)
    return hidden, grad_inner, grad_linear


def make_body(dp, tp):
    hi_count = dp // (GROUP * PAIR)

    def permute(x, target):
        pairs = []
        for d in range(dp):
            for t in range(tp):
                to_d, to_t = target(d, t)
                pairs.append((d * tp + t, to_d * tp + to_t))
        return lax.ppermute(x, AXES, pairs)

    swap_core = lambda x: permute(x, lambda d, t: (d, t ^ 1))
    swap_row = lambda x: permute(x, lambda d, t: (d, t ^ 2))
    swap_dp = lambda x, bit: permute(x, lambda d, t: (d ^ bit, t))

    def body(
        inputs,
        document,
        query_weight,
        key_weight,
        value_weight,
        gate_weight,
        out_weight,
        inner_weight,
        linear_weight,
        down_weight,
        first_gain,
        first_bias,
        head_gain,
        second_gain,
        second_bias,
        cotangent,
    ):
        rows, width = inputs.shape
        quarter = width // tp
        share = width // dp
        heads = query_weight.shape[1] // KD
        d = lax.axis_index("dp")
        t = lax.axis_index("tensor")
        core = t % 2
        row = t // 2
        low = d % PAIR
        first_head = t * heads
        projections = (query_weight, key_weight, value_weight, gate_weight)

        def joined(mine, other, place):
            return jnp.where(
                place == 0,
                jnp.concatenate([mine, other], 1),
                jnp.concatenate([other, mine], 1),
            )

        def halves(x, place):
            n = x.shape[1] // 2
            keep = lax.dynamic_slice_in_dim(x, place * n, n, 1)
            send = lax.dynamic_slice_in_dim(x, (1 - place) * n, n, 1)
            return keep, send

        def gather_columns(part):
            half = joined(part, swap_row(part), row)
            return joined(half, swap_core(half), core)

        def reduce_columns(x):
            keep, send = halves(x, core)
            x = keep + swap_core(send)
            keep, send = halves(x, row)
            return keep + swap_row(send)

        def my_columns(x):
            return lax.dynamic_slice_in_dim(x, (core * 2 + row) * quarter, quarter, 1)

        def others(part):
            blocks = [gather_columns(swap_dp(part, k * PAIR)) for k in range(1, GROUP)]
            return jnp.concatenate(blocks, 0)

        def shares(x, which):
            group = (d // PAIR) % GROUP
            cuts = [
                lax.dynamic_slice_in_dim(
                    x, ((hi * GROUP + group) * PAIR + which) * share, share, 1
                )
                for hi in range(hi_count)
            ]
            return cuts[0] if hi_count == 1 else jnp.concatenate(cuts, 1)

        def over_hi(x, axis):
            hi = d // (GROUP * PAIR)
            cut = lambda k: lax.dynamic_slice_in_dim(x, (hi ^ k) * share, share, axis)
            total = cut(0)
            for k in range(1, hi_count):
                total = total + swap_dp(cut(k), k * GROUP * PAIR)
            return total

        def summed(left, right, transposed):
            def product(which):
                a = shares(left, which)
                return tn(right, a) if transposed else tn(a, right)

            arrived = swap_dp(product(1 - low), 1)
            return over_hi(product(low) + arrived, 1 if transposed else 0)

        residual = inputs.astype(F32)
        cotangent_f = cotangent.astype(F32)
        other_inputs = others(my_columns(residual))
        other_document = jnp.stack([swap_dp(document, k * PAIR) for k in range(1, GROUP)])
        other_cotangent = others(my_columns(cotangent_f))

        first_norm, first_hat, first_inv = norm_rows(residual, first_gain, first_bias, EPS)
        normed_one = first_norm.astype(BF16)
        gated, state = retention_forward(
            normed_one, document[None], projections, head_gain, first_head
        )
        branch = reduce_columns(nn(gated, out_weight))
        middle_part = my_columns(residual) + branch
        middle = gather_columns(middle_part)
        other_middle = others(middle_part)

        second_norm, second_hat, second_inv = norm_rows(middle, second_gain, second_bias, EPS)
        normed_two = second_norm.astype(BF16)
        grad_top = cotangent_f * (document < DOCS_DEV).astype(F32)[:, None]
        grad_top_bf = grad_top.astype(BF16)
        hidden, grad_inner_bf, grad_linear_bf = mlp(
            normed_two, grad_top_bf, inner_weight, linear_weight, down_weight
        )
        upstream_two_part = reduce_columns(
            nt(grad_inner_bf, inner_weight) + nt(grad_linear_bf, linear_weight)
        )
        upstream_two = gather_columns(upstream_two_part)
        other_upstream_two = others(upstream_two_part)
        grad_middle = grad_top + norm_back(upstream_two, second_hat, second_inv, second_gain)
        grad_middle_bf = grad_middle.astype(BF16)
        grad_query_bf, grad_key_bf, grad_value_bf, grad_gates_bf, grad_normed = retention_backward(
            grad_middle_bf, state, out_weight, head_gain
        )
        upstream_one = gather_columns(
            reduce_columns(
                nt(grad_query_bf, query_weight)
                + nt(grad_key_bf, key_weight)
                + nt(grad_value_bf, value_weight)
                + nt(grad_gates_bf, gate_weight)
            )
        )
        grad_inputs = grad_middle + norm_back(upstream_one, first_hat, first_inv, first_gain)
        outputs = gather_columns(middle_part + reduce_columns(nn(hidden, down_weight)))

        other_normed_one = norm_rows(other_inputs, first_gain, first_bias, EPS)[0].astype(BF16)
        other_gated, other_state = retention_forward(
            other_normed_one, other_document, projections, head_gain, first_head
        )
        other_live = (other_document < DOCS_DEV).astype(F32).reshape(-1, 1)
        other_top = other_cotangent * other_live
        other_top_bf = other_top.astype(BF16)
        other_norm, other_hat, other_inv = norm_rows(other_middle, second_gain, second_bias, EPS)
        other_normed_two = other_norm.astype(BF16)
        other_hidden, other_inner_bf, other_linear_bf = mlp(
            other_normed_two, other_top_bf, inner_weight, linear_weight, down_weight
        )
        stack = lambda a, b: jnp.concatenate([a, b], 0)
        all_two = stack(normed_two, other_normed_two)
        all_top = stack(grad_top_bf, other_top_bf)
        grad_down = summed(all_top, stack(hidden, other_hidden), True)
        grad_inner = summed(all_two, stack(grad_inner_bf, other_inner_bf), False)
        grad_linear = summed(all_two, stack(grad_linear_bf, other_linear_bf), False)

        other_middle_bf = (
            other_top + norm_back(other_upstream_two, other_hat, other_inv, second_gain)
        ).astype(BF16)
        other_query_bf, other_key_bf, other_value_bf, other_gates_bf, unused = retention_backward(
            other_middle_bf, other_state, out_weight, head_gain
        )
        all_one = stack(normed_one, other_normed_one)
        grad_out = summed(
            stack(grad_middle_bf, other_middle_bf), stack(gated, other_gated), True
        )
        grad_gate = summed(all_one, stack(grad_gates_bf, other_gates_bf), False)
        grad_value = summed(all_one, stack(grad_value_bf, other_value_bf), False)
        grad_query = summed(all_one, stack(grad_query_bf, other_query_bf), False)
        grad_key = summed(all_one, stack(grad_key_bf, other_key_bf), False)

        sums = [
            jnp.sum(upstream_two * second_hat, 0),
            jnp.sum(upstream_two, 0),
            jnp.sum(grad_normed * state[6], 0),
            jnp.sum(upstream_one * first_hat, 0),
            jnp.sum(upstream_one, 0),
        ]
        total = jnp.concatenate(sums)
        bit = 1
        while bit < dp:
            total = total + swap_dp(total, bit)
            bit *= 2
        ends = []
        at = 0
        for s in sums:
            ends.append(total[at : at + s.shape[0]])
            at += s.shape[0]
        second_gain_sum, second_bias_sum, head_gain_sum, first_gain_sum, first_bias_sum = ends
        return (
            outputs,
            grad_inputs,
            grad_query,
            grad_key,
            grad_value,
            grad_gate,
            grad_out,
            grad_inner,
            grad_linear,
            grad_down,
            first_gain_sum,
            first_bias_sum,
            head_gain_sum,
            second_gain_sum,
            second_bias_sum,
        )

    return body


def solution(mesh):
    in_specs = (
        P("dp", None),
        P("dp"),
        P(None, "tensor"),
        P(None, "tensor"),
        P(None, "tensor"),
        P(None, "tensor"),
        P("tensor", None),
        P(None, "tensor"),
        P(None, "tensor"),
        P("tensor", None),
        P(),
        P(),
        P("tensor"),
        P(),
        P(),
        P("dp", None),
    )
    out_specs = (
        P("dp", None),
        P("dp", None),
        P("dp", "tensor"),
        P("dp", "tensor"),
        P("dp", "tensor"),
        P("dp", "tensor"),
        P("tensor", "dp"),
        P("dp", "tensor"),
        P("dp", "tensor"),
        P("tensor", "dp"),
        P(),
        P(),
        P("tensor"),
        P(),
        P(),
    )
    body = make_body(mesh.shape["dp"], mesh.shape["tensor"])
    return jax.shard_map(body, mesh=mesh, in_specs=in_specs, out_specs=out_specs, check_vma=False)
```

```python
import functools
from types import SimpleNamespace

import jax
import jax.numpy as jnp
from jax import lax
from jax.experimental import pallas as pl
from jax.experimental.pallas import tpu as pltpu
from jax.sharding import PartitionSpec as P

KD = 256
VD = 432
DOCS_DEV = 8
SIDE = 1
NEXT = 2
FAR = 4
BITS = 8

EPS = 1e-05
HEAD_EPS = 0.25
SCALE = KD ** (-0.5)

F32 = jnp.float32
BF16 = jnp.bfloat16
AXES = ("dp", "tensor")


def dot(a, b, ca, cb):
    return lax.dot_general(a, b, (((ca,), (cb,)), ((), ())), preferred_element_type=F32)


def nn(a, b):
    return dot(a, b, 1, 0)


def nt(a, b):
    return dot(a, b, 1, 1)


def tn(a, b):
    return dot(a, b, 0, 0)


def standard(value, epsilon, axis):
    center = value - jnp.mean(value, axis, keepdims=True)
    inverse = lax.rsqrt(jnp.mean(center * center, axis, keepdims=True) + epsilon)
    return center * inverse, inverse


def norm_back(upstream, unit, inverse, gain, axis):
    scaled = upstream * gain
    return inverse * (
        scaled
        - jnp.mean(scaled, axis, keepdims=True)
        - unit * jnp.mean(scaled * unit, axis, keepdims=True)
    )


class Call:
    def __init__(self, blocks):
        self.blocks = blocks
        self.keys, self.arrays, self.specs = [], [], []
        self.out_keys, self.outs, self.out_specs = [], [], []
        self.temp_keys, self.temps = [], []

    def add(self, key, array, spec):
        self.keys.append(key)
        self.arrays.append(array)
        self.specs.append(spec)

    def whole(self, **arrays):
        for key, array in arrays.items():
            spec = pl.BlockSpec(array.shape, zeros(array.ndim), pipeline_mode=pl.Buffered(1))
            self.add(key, array, spec)

    def scalars(self, **arrays):
        for key, array in arrays.items():
            self.add(key, array, pl.BlockSpec(memory_space=pltpu.SMEM))

    def cut(self, **arrays):
        for key, array in arrays.items():
            self.add(key, array, leading(array.shape[1:]))

    def pieces(self, **groups):
        for key, group in groups.items():
            for block, runs in enumerate(group):
                for run, parts in enumerate(runs):
                    for part in parts:
                        spec = pl.BlockSpec(part.shape, zeros(2), pipeline_mode=pl.Buffered(1))
                        self.add((key, block, run), part, spec)

    def after(self, *arrays):
        for array in arrays:
            self.add(None, array, pl.BlockSpec(memory_space=pl.ANY))

    def result(self, **forms):
        for key, (shape, dtype) in forms.items():
            self.out_keys.append(key)
            self.outs.append(jax.ShapeDtypeStruct(shape, dtype))
            self.out_specs.append(pl.BlockSpec(shape, zeros(len(shape))))

    def results(self, **forms):
        for key, (shape, dtype) in forms.items():
            self.out_keys.append(key)
            self.outs.append(jax.ShapeDtypeStruct((self.blocks,) + shape, dtype))
            self.out_specs.append(leading(shape))

    def temp(self, **forms):
        for key, (shape, dtype) in forms.items():
            self.temp_keys.append(key)
            self.temps.append(pltpu.VMEM(shape, dtype))

    def run(self, name, body):
        keys = self.keys + self.out_keys + self.temp_keys

        def kernel(*refs):
            r = SimpleNamespace()
            for key, ref in zip(keys, refs):
                if isinstance(key, tuple):
                    runs = r.__dict__.setdefault(key[0], {}).setdefault(key[1], {})
                    runs.setdefault(key[2], []).append(ref)
                elif key is not None:
                    setattr(r, key, ref)
            body(r)

        got = pl.pallas_call(
            kernel,
            grid=(self.blocks,),
            in_specs=self.specs,
            out_specs=self.out_specs,
            out_shape=self.outs,
            scratch_shapes=self.temps,
            cost_estimate=LIGHT,
            name=name,
        )(*self.arrays)
        return SimpleNamespace(**dict(zip(self.out_keys, got)))


LIGHT = pl.CostEstimate(flops=1, transcendentals=0, bytes_accessed=1)


def zeros(n):
    return lambda *g: (0,) * n


def leading(shape):
    rest = (0,) * len(shape)
    return pl.BlockSpec((None,) + shape, lambda b: (b,) + rest)


def place_pieces(r, target, group, width):
    core = r.info[0]
    row = r.info[1]

    def put(runs):
        first = 0
        for parts in runs.values():
            size = width // len(parts)
            if len(parts) == 4:
                far = (1 - core) * 2
                at = [core * 2 + row, core * 2 + 1 - row, far + row, far + 1 - row]
            else:
                at = [core, 1 - core]
            rows = pl.ds(first, parts[0].shape[0])
            first += parts[0].shape[0]
            for i, part in enumerate(parts):
                target[rows, pl.ds(pl.multiple_of(at[i] * size, size), size)] = part[...]

    if len(group) == 1:
        put(group[0])
    else:
        for block, runs in group.items():
            pl.when(pl.program_id(0) == block)(functools.partial(put, runs))


def downwards(r):
    across = r.document[...].astype(F32)
    rows = across.shape[1]
    return jnp.broadcast_to(across, (rows, rows)).T


def decays(r, heads):
    down = downwards(r)
    rows = down.shape[0]
    n = lax.broadcasted_iota(jnp.int32, (rows, rows), 0)
    m = lax.broadcasted_iota(jnp.int32, (rows, rows), 1)
    allowed = (n >= m) & (down == r.document[...].astype(F32))
    spread = jnp.where(allowed, (n - m).astype(F32), 0.0)
    return [jnp.where(allowed, jnp.exp(spread * r.rates[h]), 0.0) for h in range(heads)]


def quarter_columns(r, width):
    core = r.info[0]
    row = r.info[1]
    size = width // 4
    far = (1 - core) * 2
    at = [core * 2 + row, core * 2 + 1 - row, far + row, far + 1 - row]
    return [pl.ds(pl.multiple_of(a * size, size), size) for a in at]


def attend(own, name, source, document, shared, weights, heads, after=()):
    query_w, key_w, value_wt, gate_wt, out_w = weights
    blocks, unused, rows = document.shape
    width = query_w.shape[0]
    features = value_wt.shape[0]
    c = Call(blocks)
    c.scalars(info=shared.info, rates=shared.rates)
    c.whole(gain=shared.first_gain, bias=shared.first_bias, head_gain=shared.head_gain)
    c.cut(document=document)
    c.whole(qw=query_w, kw=key_w, vw=value_wt, gw=gate_wt)
    c.after(*after)
    if own:
        c.whole(x=source, ow=out_w)
        part = ((rows, width // 4), F32)
        c.result(b0=part, b1=part, b2=part, b3=part)
    else:
        c.pieces(x=source)
        c.temp(x_rows=((rows, width), F32))
    wide = ((rows, heads * KD), BF16)
    tall = ((features, rows), BF16)
    tall_f = ((features, rows), F32)
    c.results(
        normed=((rows, width), BF16),
        q=wide,
        k=wide,
        v=tall,
        s=((heads, rows, rows), BF16),
        g=tall_f,
        hat=tall_f,
        inv=((heads, 1, rows), F32),
        gated=tall,
    )

    def body(r):
        if own:
            x = r.x[...].astype(F32)
        else:
            place_pieces(r, r.x_rows, r.x, width)
            x = r.x_rows[...]
        hat, unused = standard(x, EPS, 1)
        normed = (hat * r.gain[...] + r.bias[...]).astype(BF16)
        r.normed[...] = normed
        r.q[...] = nn(normed, r.qw[...]).astype(BF16)
        r.k[...] = (nn(normed, r.kw[...]) * SCALE).astype(BF16)
        r.v[...] = nt(r.vw[...], normed).astype(BF16)
        r.g[...] = nt(r.gw[...], normed)
        decay = decays(r, heads)
        for h in range(heads):
            kd = pl.ds(h * KD, KD)
            vd = pl.ds(h * VD, VD)
            score = (nt(r.q[:, kd], r.k[:, kd]) * decay[h]).astype(BF16)
            r.s[h] = score
            head_hat, head_inv = standard(nt(r.v[vd, :], score), HEAD_EPS, 0)
            r.hat[vd, :] = head_hat
            r.inv[h] = head_inv
            gates = r.g[vd, :]
            swish = gates * jax.nn.sigmoid(gates)
            r.gated[vd, :] = (swish * (head_hat * r.head_gain[vd, :])).astype(BF16)
        if own:
            cuts = quarter_columns(r, width)
            for cut, out in zip(cuts, (r.b0, r.b1, r.b2, r.b3)):
                out[...] = tn(r.gated[...], r.ow[:, cut])
            r.b0[...] += r.x[:, cuts[0]].astype(F32)

    return c.run(name, body)


def feed(own, name, middle, top, shared, weights, after=()):
    inner_wt, linear_wt, down_w = weights
    features, width = inner_wt.shape
    blocks, rows = len(middle), shared.rows
    c = Call(blocks)
    c.scalars(info=shared.info)
    c.whole(gain=shared.second_gain, bias=shared.second_bias)
    c.pieces(m=middle)
    c.whole(iw=inner_wt, lw=linear_wt, dw=down_w)
    c.after(*after)
    c.temp(m_rows=((rows, width), F32))
    if own:
        c.whole(c=top)
        part = ((rows, width // 4), F32)
        c.result(two0=part, two1=part, two2=part, two3=part)
        c.result(ff0=part, ff1=part, ff2=part, ff3=part)
    else:
        c.pieces(c=top)
        c.temp(c_rows=((rows, width), F32))
    flat = ((rows, width), BF16)
    tall = ((features, rows), BF16)
    c.results(normed=flat, top=flat, hidden=tall, gi=tall, gl=tall)

    def body(r):
        place_pieces(r, r.m_rows, r.m, width)
        hat, unused = standard(r.m_rows[...], EPS, 1)
        r.normed[...] = (hat * r.gain[...] + r.bias[...]).astype(BF16)
        if own:
            r.top[...] = r.c[...]
        else:
            place_pieces(r, r.c_rows, r.c, width)
            r.top[...] = r.c_rows[...].astype(BF16)
        for at in range(0, features, VD):
            cut = pl.ds(at, VD)
            inner = nt(r.iw[cut, :], r.normed[...])
            linear = nt(r.lw[cut, :], r.normed[...])
            upstream = nt(r.dw[cut, :], r.top[...])
            cumulative = 0.5 * (1.0 + lax.erf(inner * 0.7071067811865476))
            gelu = inner * cumulative
            slope = cumulative + inner * jnp.exp(-0.5 * inner * inner) * 0.3989422804014327
            r.hidden[cut, :] = (gelu * linear).astype(BF16)
            r.gi[cut, :] = (upstream * linear * slope).astype(BF16)
            r.gl[cut, :] = (upstream * gelu).astype(BF16)
        if own:
            cuts = quarter_columns(r, width)
            for cut, out in zip(cuts, (r.two0, r.two1, r.two2, r.two3)):
                out[...] = tn(r.gi[...], r.iw[:, cut]) + tn(r.gl[...], r.lw[:, cut])
            for cut, out in zip(cuts, (r.ff0, r.ff1, r.ff2, r.ff3)):
                out[...] = tn(r.hidden[...], r.dw[:, cut])
            r.ff0[...] += r.m_rows[:, cuts[0]]

    return c.run(name, body)


def middle_back(middle, upstream, top, shared, after=()):
    rows, width = top.shape
    c = Call(1)
    c.scalars(info=shared.info)
    c.whole(gain=shared.second_gain, top=top)
    c.pieces(m=middle, u=upstream)
    c.after(*after)
    flat = ((rows, width), F32)
    line = ((1, width), F32)
    c.temp(m_rows=flat, u_rows=flat)
    c.result(grad=flat, half=((rows, width // 2), F32), gain_sum=line, bias_sum=line)
    c.result(quarter=((rows, width // 4), F32))

    def body(r):
        place_pieces(r, r.m_rows, r.m, width)
        place_pieces(r, r.u_rows, r.u, width)
        hat, inverse = standard(r.m_rows[...], EPS, 1)
        upstream = r.u_rows[...]
        r.gain_sum[...] = jnp.sum(upstream * hat, 0, keepdims=True)
        r.bias_sum[...] = jnp.sum(upstream, 0, keepdims=True)
        r.grad[...] = r.top[...].astype(F32) + norm_back(
            upstream, hat, inverse, r.gain[...], 1
        )
        n = width // 2
        r.half[...] = r.grad[:, pl.ds(pl.multiple_of(r.info[0] * n, n), n)]
        r.quarter[...] = r.grad[:, quarter_columns(r, width)[0]]

    return c.run("middle_back", body)


def back(own, name, grad, state, document, shared, weights, heads, after=()):
    query_w, key_w, value_wt, gate_wt, out_w = weights
    width = query_w.shape[0]
    features = value_wt.shape[0]
    blocks, unused, rows = document.shape
    c = Call(blocks)
    c.scalars(info=shared.info, rates=shared.rates)
    c.whole(head_gain=shared.head_gain)
    c.cut(document=document)
    c.cut(q=state.q, k=state.k, v=state.v, s=state.s, g=state.g, hat=state.hat, inv=state.inv)
    c.whole(ow=out_w)
    c.after(*after)
    if own:
        c.whole(m=grad, qw=query_w, kw=key_w, vw=value_wt, gw=gate_wt)
        part = ((rows, width // 4), F32)
        c.result(one0=part, one1=part, one2=part, one3=part, head_sum=((features, 1), F32))
    else:
        c.pieces(m=grad)
        c.temp(m_rows=((rows, width), F32))
    wide = ((rows, heads * KD), BF16)
    tall = ((features, rows), BF16)
    c.results(gm=((rows, width), BF16), gq=wide, gk=wide, gv=tall, gg=tall)

    def body(r):
        if own:
            r.gm[...] = r.m[...].astype(BF16)
        else:
            place_pieces(r, r.m_rows, r.m, width)
            r.gm[...] = r.m_rows[...].astype(BF16)
        decay = decays(r, heads)
        for h in range(heads):
            kd = pl.ds(h * KD, KD)
            vd = pl.ds(h * VD, VD)
            grad_gated = nt(r.ow[vd, :], r.gm[...])
            gates = r.g[vd, :]
            head_hat = r.hat[vd, :]
            gain = r.head_gain[vd, :]
            sigma = jax.nn.sigmoid(gates)
            r.gg[vd, :] = (
                grad_gated * (head_hat * gain) * sigma * (1.0 + gates * (1.0 - sigma))
            ).astype(BF16)
            grad_normed = grad_gated * (gates * sigma)
            if own:
                r.head_sum[vd, :] = jnp.sum(grad_normed * head_hat, 1, keepdims=True)
            mixed = norm_back(grad_normed, head_hat, r.inv[h], gain, 0).astype(BF16)
            masked = (tn(mixed, r.v[vd, :]) * decay[h]).astype(BF16)
            r.gv[vd, :] = nn(mixed, r.s[h]).astype(BF16)
            r.gq[:, kd] = nn(masked, r.k[:, kd]).astype(BF16)
            r.gk[:, kd] = (tn(masked, r.q[:, kd]) * SCALE).astype(BF16)
        if own:
            cuts = quarter_columns(r, width)
            for cut, out in zip(cuts, (r.one0, r.one1, r.one2, r.one3)):
                out[...] = (
                    nt(r.gq[...], r.qw[cut, :])
                    + nt(r.gk[...], r.kw[cut, :])
                    + tn(r.gv[...], r.vw[:, cut])
                    + tn(r.gg[...], r.gw[:, cut])
                )

    return c.run(name, body)


def weigh(name, terms, blocks, which, after=()):
    rows = terms[0][0].shape[0]
    arrays, specs, outs, out_specs = [], [], [], []
    before = lambda b: jnp.maximum(b - 1, 0)
    for left, lefts, right, rights, turned, size in terms:
        arrays += [left, lefts, right, rights]
        specs += [
            pl.BlockSpec((rows, size), lambda b, w: (0, w[0])),
            pl.BlockSpec((None, rows, size), lambda b, w: (before(b), 0, w[0])),
            pl.BlockSpec(right.shape, lambda b, w: (0, 0)),
            pl.BlockSpec((None,) + right.shape, lambda b, w: (before(b), 0, 0)),
        ]
        shape = (size, right.shape[1]) if turned else (right.shape[0], size)
        outs.append(jax.ShapeDtypeStruct(shape, F32))
        out_specs.append(pl.BlockSpec(shape, lambda b, w: (0, 0)))
    for array in after:
        arrays.append(array)
        specs.append(pl.BlockSpec(memory_space=pl.ANY))

    def kernel(w, *refs):
        ins = refs[: 4 * len(terms)]
        results = refs[len(arrays) :]
        b = pl.program_id(0)

        def product(i, left, right):
            return tn(left, right) if terms[i][4] else nn(right, left)

        @pl.when(b == 0)
        def _():
            for i in range(len(terms)):
                left, lefts, right, rights = ins[4 * i : 4 * i + 4]
                results[i][...] = product(i, left[...], right[...])

        @pl.when(b > 0)
        def _():
            for i in range(len(terms)):
                left, lefts, right, rights = ins[4 * i : 4 * i + 4]
                results[i][...] += product(i, lefts[...], rights[...])

    return pl.pallas_call(
        kernel,
        grid_spec=pltpu.PrefetchScalarGridSpec(
            num_scalar_prefetch=1, grid=(blocks,), in_specs=specs, out_specs=out_specs
        ),
        out_shape=outs,
        cost_estimate=LIGHT,
        name=name,
    )(which, *arrays)


def joined(pieces, info, width, after=()):
    c = Call(1)
    c.scalars(info=info)
    c.pieces(y=[[pieces]])
    c.after(*after)
    c.result(out=((pieces[0].shape[0], width), F32))
    return c.run("joined", lambda r: place_pieces(r, r.out, r.y, width)).out


def input_gradient(pieces, inputs, middle, info, gain, after=()):
    rows, width = inputs.shape
    c = Call(1)
    c.scalars(info=info)
    c.whole(gain=gain, x=inputs, middle=middle)
    c.pieces(u=[[pieces]])
    c.after(*after)
    line = ((1, width), F32)
    c.result(out=((rows, width), F32), gain_sum=line, bias_sum=line)
    c.temp(u_rows=((rows, width), F32))

    def body(r):
        place_pieces(r, r.u_rows, r.u, width)
        hat, inverse = standard(r.x[...].astype(F32), EPS, 1)
        upstream = r.u_rows[...]
        r.gain_sum[...] = jnp.sum(upstream * hat, 0, keepdims=True)
        r.bias_sum[...] = jnp.sum(upstream, 0, keepdims=True)
        r.out[...] = r.middle[...] + norm_back(upstream, hat, inverse, r.gain[...], 1)

    return c.run("finish", body)


def make_body(dp, tp):
    hi_count = dp // BITS

    def permute(x, target):
        pairs = []
        for d in range(dp):
            for t in range(tp):
                to_d, to_t = target(d, t)
                pairs.append((d * tp + t, to_d * tp + to_t))
        return lax.ppermute(x, AXES, pairs)

    swap_core = lambda x: permute(x, lambda d, t: (d, t ^ 1))
    swap_row = lambda x: permute(x, lambda d, t: (d, t ^ 2))
    swap_dp = lambda x, bit: permute(x, lambda d, t: (d ^ bit, t))

    gate = lambda x, earlier: lax.optimization_barrier((x,) + tuple(earlier))[0] if earlier else x

    class Stages:
        def __init__(self):
            self.before, self.now, self.sends = [], [], 0
            self.spare, self.fresh = [], []

        def send(self, swap, x):
            got = swap(gate(x, self.before))
            self.now.append(got)
            self.sends += 1
            return got

        def ran(self, *arrays):
            self.now += arrays

        def later(self, x):
            slot = [x, None]
            self.fresh.append(slot)
            return slot

        def end(self, limit=5):
            while self.spare and self.sends < limit:
                slot = self.spare.pop(0)
                slot[1] = self.send(swap_core, slot[0])
            self.spare, self.fresh = self.spare + self.fresh, []
            self.before, self.now, self.sends = self.now, [], 0

    def body(
        inputs,
        document,
        query_weight,
        key_weight,
        value_weight,
        gate_weight,
        out_weight,
        inner_weight,
        linear_weight,
        down_weight,
        first_gain,
        first_bias,
        head_gain,
        second_gain,
        second_bias,
        cotangent,
    ):
        rows, width = inputs.shape
        share = width // dp
        heads = query_weight.shape[1] // KD
        d = lax.axis_index("dp")
        t = lax.axis_index("tensor")
        core = t % 2
        row = t // 2
        info = jnp.stack([core, row]).astype(jnp.int32)
        numbers = (t * heads + jnp.arange(heads)).astype(F32)
        shared = SimpleNamespace(
            info=info,
            rows=rows,
            rates=jnp.log1p(-jnp.exp2(-5.0 - numbers)),
            first_gain=first_gain[None],
            first_bias=first_bias[None],
            second_gain=second_gain[None],
            second_bias=second_bias[None],
            head_gain=head_gain[:, None],
        )
        attention = (query_weight, key_weight, value_weight.T, gate_weight.T, out_weight)
        hidden_layer = (inner_weight.T, linear_weight.T, down_weight)

        low = d % BITS

        def share_of(x, place):
            cuts = [
                lax.dynamic_slice_in_dim(x, (hi * BITS + place) * share, share, x.ndim - 1)
                for hi in range(hi_count)
            ]
            return jnp.concatenate(cuts, x.ndim - 1)

        def over_hi(x, axis):
            hi = d // BITS
            cut = lambda k: lax.dynamic_slice_in_dim(x, (hi ^ k) * share, share, axis)
            total = cut(0)
            for k in range(1, hi_count):
                total = total + swap_dp(cut(k), k * BITS)
            return total

        def product(name, terms, place, after=()):
            ready = []
            for left, lefts, right, rights, turned in terms:
                if hi_count > 1:
                    left, lefts = share_of(left, place), share_of(lefts, place)
                ready.append((left, lefts, right, rights, turned, hi_count * share))
            index = place if hi_count == 1 else place * 0
            return weigh(name, ready, 4, index.reshape(1).astype(jnp.int32), after)

        def finished(mine, arrived, axis=1):
            return over_hi(mine + arrived, axis) if hi_count > 1 else mine + arrived

        def term(left, lefts, right, rights, turned=False):
            return (left[0], lefts, right[0], rights, turned)

        side = lambda x: swap_dp(x, SIDE)
        following = lambda x: swap_dp(x, NEXT)
        far = lambda x: swap_dp(x, FAR)
        stack = lambda *parts: jnp.concatenate(parts, 0)

        def half(array):
            return lax.dynamic_slice_in_dim(array, core * (width // 2), width // 2, 1).astype(F32)

        def pairs(*slots):
            return [[slot[0], slot[1]] for slot in slots]

        def quads(one, two):
            return [[one[0], two[0], one[1], two[1]]]

        own_doc = document[None, None]
        live = (document < DOCS_DEV)[:, None]
        top = jnp.where(live, cotangent, jnp.zeros((), BF16))
        top_half = half(top)
        input_half = half(inputs)
        k = rows // 4
        at = Stages()

        doc_side = at.send(side, document)
        doc_far = at.send(far, document)
        x_side = [at.later(at.send(side, input_half[: 2 * k]))]
        x_far = [at.later(at.send(far, input_half[:k]))]
        own = attend(True, "attend_own", inputs, own_doc, shared, attention, heads)
        at.ran(own.b0)
        at.end()

        branch3 = at.send(swap_core, own.b3)
        branch2 = at.send(swap_core, own.b2)
        doc_both = at.send(side, doc_far)
        at.end(0)

        branch1 = at.send(swap_row, own.b1 + branch3)
        x_side.append(at.later(at.send(side, input_half[2 * k :])))
        x_far.append(at.later(at.send(far, input_half[k : 2 * k])))
        at.end()
        middle = own.b0 + branch2 + branch1

        middle_row = at.send(swap_row, middle)
        middle_core = at.send(swap_core, middle)
        x_far.append(at.later(at.send(far, input_half[2 * k : 3 * k])))
        x_both = [at.later(at.send(side, stack(x_far[0][0], x_far[1][0])))]
        at.end()

        middle_cross = at.send(swap_core, middle_row)
        at.end(3)

        middle_own = [quads([middle, middle_core], [middle_row, middle_cross])]
        x_far.append(at.later(at.send(far, input_half[3 * k :])))
        m_next = at.later(at.send(following, middle))
        fed = feed(True, "feed_own", middle_own, top, shared, hidden_layer, at.before)
        at.ran(fed.two0)
        at.end()

        two3 = at.send(swap_core, fed.two3)
        two2 = at.send(swap_core, fed.two2)
        at.end(3)

        two1 = at.send(swap_row, fed.two1 + two3)
        x_both.append(at.later(at.send(side, stack(x_far[2][0], x_far[3][0]))))
        m_far = at.send(far, middle[: 2 * k])
        at.end()
        two = fed.two0 + two2 + two1

        two_row = at.send(swap_row, two)
        two_core = at.send(swap_core, two)
        m_far = stack(m_far, at.send(far, middle[2 * k :]))
        at.end()
        m_far = at.later(m_far)

        two_cross = at.send(swap_core, two_row)
        at.end(3)

        two_own = [quads([two, two_core], [two_row, two_cross])]
        grad = middle_back(middle_own, two_own, top, shared, at.before)
        at.ran(grad.grad)
        at.end(1)

        g_side = at.later(at.send(side, grad.half))
        g_far = at.later(at.send(far, grad.quarter))
        m_next_row = at.later(at.send(swap_row, m_next[0]))
        t_next = [at.later(at.send(following, top_half[: 2 * k]))]
        other_doc = jnp.stack([doc_side, doc_far, doc_both])[:, None]
        others = attend(
            False,
            "attend",
            [pairs(*x_side), pairs(*x_far), pairs(*x_both)],
            other_doc,
            shared,
            attention,
            heads,
            at.before,
        )
        at.ran(others.q)
        at.end()

        g_both = at.later(at.send(side, g_far[0]))
        g_far_row = at.later(at.send(swap_row, g_far[0]))
        t_far = [at.later(at.send(far, top_half[: k + k // 2]))]
        backed = back(
            True, "back_own", grad.grad, own, own_doc, shared, attention, heads, at.before
        )
        at.ran(backed.one0)
        at.end()

        g_both_row = at.later(at.send(swap_row, g_both[0]))
        t_far.append(at.later(at.send(far, top_half[k + k // 2 : 2 * k + k // 2])))
        t_next.append(at.later(at.send(following, top_half[2 * k :])))
        at.end()
        at.end()

        t_far.append(at.later(at.send(far, top_half[2 * k + k // 2 :])))
        m_far_row = at.later(at.send(swap_row, m_far[0]))
        m_both = at.later(at.send(following, m_far[0]))
        other_backed = back(
            False,
            "back",
            [pairs(g_side), quads(g_far, g_far_row), quads(g_both, g_both_row)],
            others,
            other_doc,
            shared,
            attention,
            heads,
            at.before,
        )
        at.ran(other_backed.gq)
        at.end()

        value_terms = [
            term(backed.gm, other_backed.gm, own.gated, others.gated),
            term(own.normed, others.normed, backed.gg, other_backed.gg),
            term(own.normed, others.normed, backed.gv, other_backed.gv),
        ]
        key_terms = [
            term(own.normed, others.normed, backed.gq, other_backed.gq, True),
            term(own.normed, others.normed, backed.gk, other_backed.gk, True),
        ]
        m_both_row = at.later(at.send(swap_row, m_both[0]))
        t_both = [at.later(at.send(following, stack(t_far[0][0], t_far[1][0], t_far[2][0])))]
        value_sent = product("value_partial", value_terms, low ^ NEXT, at.before)
        key_sent = product("key_partial", key_terms, low ^ NEXT, at.before)
        at.ran(value_sent[0], key_sent[0])
        at.end()
        at.end()

        value_came = [at.send(following, value_sent[0])]
        one3 = at.send(swap_core, backed.one3)
        one2 = at.send(swap_core, backed.one2)
        other_fed = feed(
            False,
            "feed",
            [quads(m_next, m_next_row), quads(m_far, m_far_row), quads(m_both, m_both_row)],
            [pairs(*t_next), pairs(*t_far), pairs(*t_both)],
            shared,
            hidden_layer,
            at.before,
        )
        at.ran(other_fed.gi)
        at.end()

        mlp_terms = [
            term(fed.top, other_fed.top, fed.hidden, other_fed.hidden),
            term(fed.normed, other_fed.normed, fed.gi, other_fed.gi),
            term(fed.normed, other_fed.normed, fed.gl, other_fed.gl),
        ]
        one1 = at.send(swap_row, backed.one1 + one3)
        ff3 = at.send(swap_core, fed.ff3)
        ff2 = at.send(swap_core, fed.ff2)
        mlp_sent = product("mlp_partial", mlp_terms, low ^ SIDE, at.before)
        at.ran(mlp_sent[0])
        at.end()
        one = backed.one0 + one2 + one1

        value_came.append(at.send(following, value_sent[1]))
        mlp_came = [at.send(side, mlp_sent[0])]
        one_row = at.send(swap_row, one)
        one_core = at.send(swap_core, one)
        value_mine = product("value_mine", value_terms, low, at.before)
        key_mine = product("key_mine", key_terms, low, at.before)
        at.ran(value_mine[0], key_mine[0])
        at.end()

        value_came.append(at.send(following, value_sent[2]))
        mlp_came.append(at.send(side, mlp_sent[1]))
        ff1 = at.send(swap_row, fed.ff1 + ff3)
        one_cross = at.send(swap_core, one_row)
        mlp_mine = product("mlp_mine", mlp_terms, low, at.before)
        at.ran(mlp_mine[0])
        at.end()
        ff = fed.ff0 + ff2 + ff1

        mlp_came.append(at.send(side, mlp_sent[2]))
        key_came = [at.send(following, x) for x in key_sent]
        ff_row = at.send(swap_row, ff)
        ff_core = at.send(swap_core, ff)
        finish = input_gradient(
            [one, one_row, one_core, one_cross],
            inputs,
            grad.grad,
            info,
            shared.first_gain,
            at.before,
        )
        at.ran(finish.out)
        at.end()
        ff_cross = at.send(swap_core, ff_row)
        outputs = joined([ff, ff_row, ff_core, ff_cross], info, width)
        grad_down, grad_inner, grad_linear = map(finished, mlp_mine, mlp_came)
        grad_out, grad_gate, grad_value = map(finished, value_mine, value_came)
        grad_query, grad_key = [finished(a, b, 0) for a, b in zip(key_mine, key_came)]

        sums = jnp.concatenate(
            [
                grad.gain_sum[0],
                grad.bias_sum[0],
                finish.gain_sum[0],
                finish.bias_sum[0],
                backed.head_sum[:, 0],
            ]
        )
        bit = 1
        while bit < dp:
            sums = sums + swap_dp(sums, bit)
            bit *= 2
        vector = lambda i: sums[i * width : (i + 1) * width]
        return (
            outputs,
            finish.out,
            grad_query,
            grad_key,
            grad_value.T,
            grad_gate.T,
            grad_out,
            grad_inner.T,
            grad_linear.T,
            grad_down,
            vector(2),
            vector(3),
            sums[4 * width :],
            vector(0),
            vector(1),
        )

    return body


def solution(mesh):
    in_specs = (
        P("dp", None),
        P("dp"),
        P(None, "tensor"),
        P(None, "tensor"),
        P(None, "tensor"),
        P(None, "tensor"),
        P("tensor", None),
        P(None, "tensor"),
        P(None, "tensor"),
        P("tensor", None),
        P(),
        P(),
        P("tensor"),
        P(),
        P(),
        P("dp", None),
    )
    out_specs = (
        P("dp", None),
        P("dp", None),
        P("dp", "tensor"),
        P("dp", "tensor"),
        P("dp", "tensor"),
        P("dp", "tensor"),
        P("tensor", "dp"),
        P("dp", "tensor"),
        P("dp", "tensor"),
        P("tensor", "dp"),
        P(),
        P(),
        P("tensor"),
        P(),
        P(),
    )
    body = make_body(mesh.shape["dp"], mesh.shape["tensor"])
    return jax.shard_map(body, mesh=mesh, in_specs=in_specs, out_specs=out_specs, check_vma=False)
```

```python
import functools
from types import SimpleNamespace

import jax
import jax.numpy as jnp
from jax import lax
from jax.experimental import pallas as pl
from jax.experimental.pallas import tpu as pltpu
from jax.sharding import PartitionSpec as P

KD = 256
VD = 432
DOCS_DEV = 8
SIDE = 1
NEXT = 2
FAR = 4
BITS = 8

EPS = 1e-05
HEAD_EPS = 0.25
SCALE = KD ** (-0.5)

F32 = jnp.float32
BF16 = jnp.bfloat16
AXES = ("dp", "tensor")


def dot(a, b, ca, cb):
    return lax.dot_general(a, b, (((ca,), (cb,)), ((), ())), preferred_element_type=F32)


def nn(a, b):
    return dot(a, b, 1, 0)


def nt(a, b):
    return dot(a, b, 1, 1)


def tn(a, b):
    return dot(a, b, 0, 0)


def standard(value, epsilon, axis):
    center = value - jnp.mean(value, axis, keepdims=True)
    inverse = lax.rsqrt(jnp.mean(center * center, axis, keepdims=True) + epsilon)
    return center * inverse, inverse


def norm_back(upstream, unit, inverse, gain, axis):
    scaled = upstream * gain
    return inverse * (
        scaled
        - jnp.mean(scaled, axis, keepdims=True)
        - unit * jnp.mean(scaled * unit, axis, keepdims=True)
    )


class Call:
    def __init__(self, blocks):
        self.blocks = blocks
        self.keys, self.arrays, self.specs = [], [], []
        self.out_keys, self.outs, self.out_specs = [], [], []
        self.temp_keys, self.temps = [], []

    def add(self, key, array, spec):
        self.keys.append(key)
        self.arrays.append(array)
        self.specs.append(spec)

    def whole(self, **arrays):
        for key, array in arrays.items():
            spec = pl.BlockSpec(array.shape, zeros(array.ndim), pipeline_mode=pl.Buffered(1))
            self.add(key, array, spec)

    def scalars(self, **arrays):
        for key, array in arrays.items():
            self.add(key, array, pl.BlockSpec(memory_space=pltpu.SMEM))

    def cut(self, **arrays):
        for key, array in arrays.items():
            self.add(key, array, leading(array.shape[1:]))

    def pieces(self, **groups):
        for key, group in groups.items():
            for block, runs in enumerate(group):
                for run, parts in enumerate(runs):
                    for part in parts:
                        spec = pl.BlockSpec(part.shape, zeros(2), pipeline_mode=pl.Buffered(1))
                        self.add((key, block, run), part, spec)

    def after(self, *arrays):
        for array in arrays:
            self.add(None, array, pl.BlockSpec(memory_space=pl.ANY))

    def result(self, **forms):
        for key, (shape, dtype) in forms.items():
            self.out_keys.append(key)
            self.outs.append(jax.ShapeDtypeStruct(shape, dtype))
            self.out_specs.append(pl.BlockSpec(shape, zeros(len(shape))))

    def results(self, **forms):
        for key, (shape, dtype) in forms.items():
            self.out_keys.append(key)
            self.outs.append(jax.ShapeDtypeStruct((self.blocks,) + shape, dtype))
            self.out_specs.append(leading(shape))

    def temp(self, **forms):
        for key, (shape, dtype) in forms.items():
            self.temp_keys.append(key)
            self.temps.append(pltpu.VMEM(shape, dtype))

    def run(self, name, body):
        keys = self.keys + self.out_keys + self.temp_keys

        def kernel(*refs):
            r = SimpleNamespace()
            for key, ref in zip(keys, refs):
                if isinstance(key, tuple):
                    runs = r.__dict__.setdefault(key[0], {}).setdefault(key[1], {})
                    runs.setdefault(key[2], []).append(ref)
                elif key is not None:
                    setattr(r, key, ref)
            body(r)

        got = pl.pallas_call(
            kernel,
            grid=(self.blocks,),
            in_specs=self.specs,
            out_specs=self.out_specs,
            out_shape=self.outs,
            scratch_shapes=self.temps,
            cost_estimate=LIGHT,
            name=name,
        )(*self.arrays)
        return SimpleNamespace(**dict(zip(self.out_keys, got)))


LIGHT = pl.CostEstimate(flops=1, transcendentals=0, bytes_accessed=1)


def zeros(n):
    return lambda *g: (0,) * n


def leading(shape):
    rest = (0,) * len(shape)
    return pl.BlockSpec((None,) + shape, lambda b: (b,) + rest)


def place_pieces(r, target, group, width):
    core = r.info[0]
    row = r.info[1]

    def put(runs):
        first = 0
        for parts in runs.values():
            size = width // len(parts)
            if len(parts) == 4:
                far = (1 - core) * 2
                at = [core * 2 + row, core * 2 + 1 - row, far + row, far + 1 - row]
            else:
                at = [core, 1 - core]
            rows = pl.ds(first, parts[0].shape[0])
            first += parts[0].shape[0]
            for i, part in enumerate(parts):
                target[rows, pl.ds(pl.multiple_of(at[i] * size, size), size)] = part[...]

    if len(group) == 1:
        put(group[0])
    else:
        for block, runs in group.items():
            pl.when(pl.program_id(0) == block)(functools.partial(put, runs))


def downwards(r):
    across = r.document[...].astype(F32)
    rows = across.shape[1]
    return jnp.broadcast_to(across, (rows, rows)).T


def decays(r, heads):
    down = downwards(r)
    rows = down.shape[0]
    n = lax.broadcasted_iota(jnp.int32, (rows, rows), 0)
    m = lax.broadcasted_iota(jnp.int32, (rows, rows), 1)
    allowed = (n >= m) & (down == r.document[...].astype(F32))
    spread = jnp.where(allowed, (n - m).astype(F32), 0.0)
    return [jnp.where(allowed, jnp.exp(spread * r.rates[h]), 0.0) for h in range(heads)]


def half_columns(r, width):
    size = width // 2
    return [pl.ds(pl.multiple_of(a * size, size), size) for a in (r.info[0], 1 - r.info[0])]


def attend(own, name, source, document, shared, weights, heads, after=()):
    query_w, key_w, value_wt, gate_wt, out_w = weights
    blocks, unused, rows = document.shape
    width = query_w.shape[0]
    features = value_wt.shape[0]
    c = Call(blocks)
    c.scalars(info=shared.info, rates=shared.rates)
    c.whole(gain=shared.first_gain, bias=shared.first_bias, head_gain=shared.head_gain)
    c.cut(document=document)
    c.whole(qw=query_w, kw=key_w, vw=value_wt, gw=gate_wt)
    c.after(*after)
    if own:
        c.whole(x=source, ow=out_w)
        part = ((rows, width // 2), F32)
        c.result(near=part, away=part)
    else:
        c.pieces(x=source)
        c.temp(x_rows=((rows, width), F32))
    wide = ((rows, heads * KD), BF16)
    tall = ((features, rows), BF16)
    tall_f = ((features, rows), F32)
    c.results(
        normed=((rows, width), BF16),
        q=wide,
        k=wide,
        v=tall,
        s=((heads, rows, rows), BF16),
        g=tall_f,
        hat=tall_f,
        inv=((heads, 1, rows), F32),
        gated=tall,
    )

    def body(r):
        if own:
            x = r.x[...].astype(F32)
        else:
            place_pieces(r, r.x_rows, r.x, width)
            x = r.x_rows[...]
        hat, unused = standard(x, EPS, 1)
        normed = (hat * r.gain[...] + r.bias[...]).astype(BF16)
        r.normed[...] = normed
        r.q[...] = nn(normed, r.qw[...]).astype(BF16)
        r.k[...] = (nn(normed, r.kw[...]) * SCALE).astype(BF16)
        r.v[...] = nt(r.vw[...], normed).astype(BF16)
        r.g[...] = nt(r.gw[...], normed)
        decay = decays(r, heads)
        for h in range(heads):
            kd = pl.ds(h * KD, KD)
            vd = pl.ds(h * VD, VD)
            score = (nt(r.q[:, kd], r.k[:, kd]) * decay[h]).astype(BF16)
            r.s[h] = score
            head_hat, head_inv = standard(nt(r.v[vd, :], score), HEAD_EPS, 0)
            r.hat[vd, :] = head_hat
            r.inv[h] = head_inv
            gates = r.g[vd, :]
            swish = gates * jax.nn.sigmoid(gates)
            r.gated[vd, :] = (swish * (head_hat * r.head_gain[vd, :])).astype(BF16)
        if own:
            for cut, out in zip(half_columns(r, width), (r.near, r.away)):
                out[...] = tn(r.gated[...], r.ow[:, cut])

    return c.run(name, body)


def feed(own, name, middle, top, shared, weights, after=()):
    inner_wt, linear_wt, down_w = weights
    features, width = inner_wt.shape
    blocks, rows = len(middle), shared.rows
    c = Call(blocks)
    c.scalars(info=shared.info)
    c.whole(gain=shared.second_gain, bias=shared.second_bias)
    c.pieces(m=middle)
    c.whole(iw=inner_wt, lw=linear_wt, dw=down_w)
    c.after(*after)
    c.temp(m_rows=((rows, width), F32))
    if own:
        c.whole(c=top)
        part = ((rows, width // 2), F32)
        c.result(two_near=part, two_away=part, ff_near=part, ff_away=part)
    else:
        c.pieces(c=top)
        c.temp(c_rows=((rows, width), F32))
    flat = ((rows, width), BF16)
    tall = ((features, rows), BF16)
    c.results(normed=flat, top=flat, hidden=tall, gi=tall, gl=tall)

    def body(r):
        place_pieces(r, r.m_rows, r.m, width)
        hat, unused = standard(r.m_rows[...], EPS, 1)
        r.normed[...] = (hat * r.gain[...] + r.bias[...]).astype(BF16)
        if own:
            r.top[...] = r.c[...]
        else:
            place_pieces(r, r.c_rows, r.c, width)
            r.top[...] = r.c_rows[...].astype(BF16)
        for at in range(0, features, VD):
            cut = pl.ds(at, VD)
            inner = nt(r.iw[cut, :], r.normed[...])
            linear = nt(r.lw[cut, :], r.normed[...])
            upstream = nt(r.dw[cut, :], r.top[...])
            cumulative = 0.5 * (1.0 + lax.erf(inner * 0.7071067811865476))
            gelu = inner * cumulative
            slope = cumulative + inner * jnp.exp(-0.5 * inner * inner) * 0.3989422804014327
            r.hidden[cut, :] = (gelu * linear).astype(BF16)
            r.gi[cut, :] = (upstream * linear * slope).astype(BF16)
            r.gl[cut, :] = (upstream * gelu).astype(BF16)
        if own:
            cuts = half_columns(r, width)
            for cut, out in zip(cuts, (r.two_near, r.two_away)):
                out[...] = tn(r.gi[...], r.iw[:, cut]) + tn(r.gl[...], r.lw[:, cut])
            for cut, out in zip(cuts, (r.ff_near, r.ff_away)):
                out[...] = tn(r.hidden[...], r.dw[:, cut])

    return c.run(name, body)


def middle_back(middle, upstream, top, shared, after=()):
    rows, width = top.shape
    c = Call(1)
    c.scalars(info=shared.info)
    c.whole(gain=shared.second_gain, top=top)
    c.pieces(m=middle, u=upstream)
    c.after(*after)
    flat = ((rows, width), F32)
    line = ((1, width), F32)
    c.temp(m_rows=flat, u_rows=flat)
    c.result(grad=flat, half=((rows, width // 2), F32), gain_sum=line, bias_sum=line)
    c.result(quarter=((rows, width // 4), F32))

    def body(r):
        place_pieces(r, r.m_rows, r.m, width)
        place_pieces(r, r.u_rows, r.u, width)
        hat, inverse = standard(r.m_rows[...], EPS, 1)
        upstream = r.u_rows[...]
        r.gain_sum[...] = jnp.sum(upstream * hat, 0, keepdims=True)
        r.bias_sum[...] = jnp.sum(upstream, 0, keepdims=True)
        r.grad[...] = r.top[...].astype(F32) + norm_back(
            upstream, hat, inverse, r.gain[...], 1
        )
        r.half[...] = r.grad[:, half_columns(r, width)[0]]
        n = width // 4
        at = (r.info[0] * 2 + r.info[1]) * n
        r.quarter[...] = r.grad[:, pl.ds(pl.multiple_of(at, n), n)]

    return c.run("middle_back", body)


def back(own, name, grad, state, document, shared, weights, heads, after=()):
    query_w, key_w, value_wt, gate_wt, out_w = weights
    width = query_w.shape[0]
    features = value_wt.shape[0]
    blocks, unused, rows = document.shape
    c = Call(blocks)
    c.scalars(info=shared.info, rates=shared.rates)
    c.whole(head_gain=shared.head_gain)
    c.cut(document=document)
    c.cut(q=state.q, k=state.k, v=state.v, s=state.s, g=state.g, hat=state.hat, inv=state.inv)
    c.whole(ow=out_w)
    c.after(*after)
    if own:
        c.whole(m=grad, qw=query_w, kw=key_w, vw=value_wt, gw=gate_wt)
        part = ((rows, width // 2), F32)
        c.result(near=part, away=part, head_sum=((features, 1), F32))
    else:
        c.pieces(m=grad)
        c.temp(m_rows=((rows, width), F32))
    wide = ((rows, heads * KD), BF16)
    tall = ((features, rows), BF16)
    c.results(gm=((rows, width), BF16), gq=wide, gk=wide, gv=tall, gg=tall)

    def body(r):
        if own:
            r.gm[...] = r.m[...].astype(BF16)
        else:
            place_pieces(r, r.m_rows, r.m, width)
            r.gm[...] = r.m_rows[...].astype(BF16)
        decay = decays(r, heads)
        for h in range(heads):
            kd = pl.ds(h * KD, KD)
            vd = pl.ds(h * VD, VD)
            grad_gated = nt(r.ow[vd, :], r.gm[...])
            gates = r.g[vd, :]
            head_hat = r.hat[vd, :]
            gain = r.head_gain[vd, :]
            sigma = jax.nn.sigmoid(gates)
            r.gg[vd, :] = (
                grad_gated * (head_hat * gain) * sigma * (1.0 + gates * (1.0 - sigma))
            ).astype(BF16)
            grad_normed = grad_gated * (gates * sigma)
            if own:
                r.head_sum[vd, :] = jnp.sum(grad_normed * head_hat, 1, keepdims=True)
            mixed = norm_back(grad_normed, head_hat, r.inv[h], gain, 0).astype(BF16)
            masked = (tn(mixed, r.v[vd, :]) * decay[h]).astype(BF16)
            r.gv[vd, :] = nn(mixed, r.s[h]).astype(BF16)
            r.gq[:, kd] = nn(masked, r.k[:, kd]).astype(BF16)
            r.gk[:, kd] = (tn(masked, r.q[:, kd]) * SCALE).astype(BF16)
        if own:
            for cut, out in zip(half_columns(r, width), (r.near, r.away)):
                out[...] = (
                    nt(r.gq[...], r.qw[cut, :])
                    + nt(r.gk[...], r.kw[cut, :])
                    + tn(r.gv[...], r.vw[:, cut])
                    + tn(r.gg[...], r.gw[:, cut])
                )

    return c.run(name, body)


def weigh(name, terms, blocks, which, after=()):
    rows = terms[0][0].shape[0]
    arrays, specs, outs, out_specs = [], [], [], []
    before = lambda b: jnp.maximum(b - 1, 0)
    for left, lefts, right, rights, turned, size in terms:
        arrays += [left, lefts, right, rights]
        specs += [
            pl.BlockSpec((rows, size), lambda b, w: (0, w[0])),
            pl.BlockSpec((None, rows, size), lambda b, w: (before(b), 0, w[0])),
            pl.BlockSpec(right.shape, lambda b, w: (0, 0)),
            pl.BlockSpec((None,) + right.shape, lambda b, w: (before(b), 0, 0)),
        ]
        shape = (size, right.shape[1]) if turned else (right.shape[0], size)
        outs.append(jax.ShapeDtypeStruct(shape, F32))
        out_specs.append(pl.BlockSpec(shape, lambda b, w: (0, 0)))
    for array in after:
        arrays.append(array)
        specs.append(pl.BlockSpec(memory_space=pl.ANY))

    def kernel(w, *refs):
        ins = refs[: 4 * len(terms)]
        results = refs[len(arrays) :]
        b = pl.program_id(0)

        def product(i, left, right):
            return tn(left, right) if terms[i][4] else nn(right, left)

        @pl.when(b == 0)
        def _():
            for i in range(len(terms)):
                left, lefts, right, rights = ins[4 * i : 4 * i + 4]
                results[i][...] = product(i, left[...], right[...])

        @pl.when(b > 0)
        def _():
            for i in range(len(terms)):
                left, lefts, right, rights = ins[4 * i : 4 * i + 4]
                results[i][...] += product(i, lefts[...], rights[...])

    return pl.pallas_call(
        kernel,
        grid_spec=pltpu.PrefetchScalarGridSpec(
            num_scalar_prefetch=1, grid=(blocks,), in_specs=specs, out_specs=out_specs
        ),
        out_shape=outs,
        cost_estimate=LIGHT,
        name=name,
    )(which, *arrays)


def joined(pieces, info, width, after=()):
    c = Call(1)
    c.scalars(info=info)
    c.pieces(y=[[pieces]])
    c.after(*after)
    c.result(out=((pieces[0].shape[0], width), F32))
    return c.run("joined", lambda r: place_pieces(r, r.out, r.y, width)).out


def input_gradient(pieces, inputs, middle, info, gain, after=()):
    rows, width = inputs.shape
    c = Call(1)
    c.scalars(info=info)
    c.whole(gain=gain, x=inputs, middle=middle)
    c.pieces(u=[[pieces]])
    c.after(*after)
    line = ((1, width), F32)
    c.result(out=((rows, width), F32), gain_sum=line, bias_sum=line)
    c.temp(u_rows=((rows, width), F32))

    def body(r):
        place_pieces(r, r.u_rows, r.u, width)
        hat, inverse = standard(r.x[...].astype(F32), EPS, 1)
        upstream = r.u_rows[...]
        r.gain_sum[...] = jnp.sum(upstream * hat, 0, keepdims=True)
        r.bias_sum[...] = jnp.sum(upstream, 0, keepdims=True)
        r.out[...] = r.middle[...] + norm_back(upstream, hat, inverse, r.gain[...], 1)

    return c.run("finish", body)


def make_body(dp, tp):
    hi_count = dp // BITS

    def permute(x, target):
        pairs = []
        for d in range(dp):
            for t in range(tp):
                to_d, to_t = target(d, t)
                pairs.append((d * tp + t, to_d * tp + to_t))
        return lax.ppermute(x, AXES, pairs)

    swap_core = lambda x: permute(x, lambda d, t: (d, t ^ 1))
    swap_row = lambda x: permute(x, lambda d, t: (d, t ^ 2))
    swap_dp = lambda x, bit: permute(x, lambda d, t: (d ^ bit, t))

    gate = lambda x, earlier: lax.optimization_barrier((x,) + tuple(earlier))[0] if earlier else x

    class Stages:
        def __init__(self):
            self.before, self.now, self.sends = [], [], 0
            self.spare, self.fresh = [], []

        def send(self, swap, x):
            got = swap(gate(x, self.before))
            self.now.append(got)
            self.sends += 1
            return got

        def ran(self, *arrays):
            self.now += arrays

        def later(self, x):
            slot = [x, None]
            self.fresh.append(slot)
            return slot

        def end(self, limit=5):
            while self.spare and self.sends < limit:
                slot = self.spare.pop(0)
                slot[1] = self.send(swap_core, slot[0])
            self.spare, self.fresh = self.spare + self.fresh, []
            self.before, self.now, self.sends = self.now, [], 0

    def body(
        inputs,
        document,
        query_weight,
        key_weight,
        value_weight,
        gate_weight,
        out_weight,
        inner_weight,
        linear_weight,
        down_weight,
        first_gain,
        first_bias,
        head_gain,
        second_gain,
        second_bias,
        cotangent,
    ):
        rows, width = inputs.shape
        share = width // dp
        heads = query_weight.shape[1] // KD
        d = lax.axis_index("dp")
        t = lax.axis_index("tensor")
        core = t % 2
        row = t // 2
        info = jnp.stack([core, row]).astype(jnp.int32)
        numbers = (t * heads + jnp.arange(heads)).astype(F32)
        shared = SimpleNamespace(
            info=info,
            rows=rows,
            rates=jnp.log1p(-jnp.exp2(-5.0 - numbers)),
            first_gain=first_gain[None],
            first_bias=first_bias[None],
            second_gain=second_gain[None],
            second_bias=second_bias[None],
            head_gain=head_gain[:, None],
        )
        attention = (query_weight, key_weight, value_weight.T, gate_weight.T, out_weight)
        hidden_layer = (inner_weight.T, linear_weight.T, down_weight)

        low = d % BITS

        def share_of(x, place):
            cuts = [
                lax.dynamic_slice_in_dim(x, (hi * BITS + place) * share, share, x.ndim - 1)
                for hi in range(hi_count)
            ]
            return jnp.concatenate(cuts, x.ndim - 1)

        def over_hi(x, axis):
            hi = d // BITS
            cut = lambda k: lax.dynamic_slice_in_dim(x, (hi ^ k) * share, share, axis)
            total = cut(0)
            for k in range(1, hi_count):
                total = total + swap_dp(cut(k), k * BITS)
            return total

        def product(name, terms, place, after=()):
            ready = []
            for left, lefts, right, rights, turned in terms:
                if hi_count > 1:
                    left, lefts = share_of(left, place), share_of(lefts, place)
                ready.append((left, lefts, right, rights, turned, hi_count * share))
            index = place if hi_count == 1 else place * 0
            return weigh(name, ready, 4, index.reshape(1).astype(jnp.int32), after)

        def finished(mine, arrived, axis=1):
            return over_hi(mine + arrived, axis) if hi_count > 1 else mine + arrived

        def term(left, lefts, right, rights, turned=False):
            return (left[0], lefts, right[0], rights, turned)

        side = lambda x: swap_dp(x, SIDE)
        following = lambda x: swap_dp(x, NEXT)
        far = lambda x: swap_dp(x, FAR)
        stack = lambda *parts: jnp.concatenate(parts, 0)

        def half(array):
            return lax.dynamic_slice_in_dim(array, core * (width // 2), width // 2, 1).astype(F32)

        def quarter(halved):
            return lax.dynamic_slice_in_dim(halved, row * (width // 4), width // 4, 1)

        def pairs(*slots):
            return [[slot[0], slot[1]] for slot in slots]

        def quads(one, two):
            return [[one[0], two[0], one[1], two[1]]]

        own_doc = document[None, None]
        live = (document < DOCS_DEV)[:, None]
        top = jnp.where(live, cotangent, jnp.zeros((), BF16))
        top_quarter = quarter(half(top))
        input_half = half(inputs)
        k = rows // 4
        at = Stages()

        doc_side = at.send(side, document)
        doc_far = at.send(far, document)
        x_side = [at.later(at.send(side, input_half[: 2 * k]))]
        t_next = at.later(at.send(following, top_quarter))
        x_far = [None, at.later(at.send(far, input_half[2 * k : 3 * k]))]
        own = attend(True, "attend_own", inputs, own_doc, shared, attention, heads)
        at.ran(own.near)
        at.end(0)

        branch = own.near + at.send(swap_core, own.away)
        at.end(2)

        branch_row = at.send(swap_row, branch)
        doc_both = at.send(side, doc_far)
        x_side.append(at.later(at.send(side, input_half[2 * k :])))
        x_far[0] = at.later(at.send(far, input_half[: 2 * k]))
        at.end()
        middle = input_half + (branch + branch_row)

        middle_core = at.send(swap_core, middle)
        at.end(3)

        x_far.append(at.later(at.send(far, input_half[3 * k :])))
        x_both = [at.later(at.send(side, x_far[0][0]))]
        t_next_row = at.later(at.send(swap_row, t_next[0]))
        middle_own = [[[middle, middle_core]]]
        fed = feed(True, "feed_own", middle_own, top, shared, hidden_layer, at.before)
        at.ran(fed.two_near)
        at.end()

        two = fed.two_near + at.send(swap_core, fed.two_away)
        at.end(2)

        two_row = at.send(swap_row, two)
        m_next = at.later(at.send(following, quarter(middle)))
        m_far = at.later(at.send(far, quarter(middle)))
        x_both.append(at.later(at.send(side, stack(x_far[1][0], x_far[2][0]))))
        at.end()
        two = two + two_row

        two_core = at.send(swap_core, two)
        at.end(3)

        grad = middle_back(middle_own, [[[two, two_core]]], top, shared, at.before)
        at.ran(grad.grad)
        at.end(9)

        g_side = at.later(at.send(side, grad.half))
        m_both = at.later(at.send(following, m_far[0]))
        g_far = at.later(at.send(far, grad.quarter))
        m_next_row = at.later(at.send(swap_row, m_next[0]))
        m_far_row = at.later(at.send(swap_row, m_far[0]))
        other_doc = jnp.stack([doc_side, doc_far, doc_both])[:, None]
        others = attend(
            False,
            "attend",
            [pairs(*x_side), pairs(*x_far), pairs(*x_both)],
            other_doc,
            shared,
            attention,
            heads,
            at.before,
        )
        at.ran(others.q)
        at.end()

        g_both = at.later(at.send(side, g_far[0]))
        g_far_row = at.later(at.send(swap_row, g_far[0]))
        t_far = at.send(far, top_quarter[: 2 * k])
        backed = back(
            True, "back_own", grad.grad, own, own_doc, shared, attention, heads, at.before
        )
        at.ran(backed.near)
        at.end()

        g_both_row = at.send(swap_row, g_both[0])
        t_far = stack(t_far, at.send(far, top_quarter[2 * k :]))
        one = backed.near + at.send(swap_core, backed.away)
        at.end()
        t_far = at.later(t_far)

        g_both_row = [g_both_row, at.send(swap_core, g_both_row)]
        at.end(4)

        t_both = at.later(at.send(following, t_far[0]))
        m_both_row = at.later(at.send(swap_row, m_both[0]))
        t_far_row = at.later(at.send(swap_row, t_far[0]))
        other_backed = back(
            False,
            "back",
            [pairs(g_side), quads(g_far, g_far_row), quads(g_both, g_both_row)],
            others,
            other_doc,
            shared,
            attention,
            heads,
            at.before,
        )
        at.ran(other_backed.gq)
        at.end()

        value_terms = [
            term(backed.gm, other_backed.gm, own.gated, others.gated),
            term(own.normed, others.normed, backed.gg, other_backed.gg),
            term(own.normed, others.normed, backed.gv, other_backed.gv),
        ]
        key_terms = [
            term(own.normed, others.normed, backed.gq, other_backed.gq, True),
            term(own.normed, others.normed, backed.gk, other_backed.gk, True),
        ]
        t_both_row = at.send(swap_row, t_both[0])
        ff = fed.ff_near + at.send(swap_core, fed.ff_away)
        value_sent = product("value_partial", value_terms, low ^ NEXT, at.before)
        key_sent = product("key_partial", key_terms, low ^ NEXT, at.before)
        at.ran(value_sent[0], key_sent[0])
        at.end()

        t_both_row = [t_both_row, at.send(swap_core, t_both_row)]
        at.end(4)

        value_came = [at.send(following, value_sent[0])]
        key_came = [at.send(following, key_sent[0])]
        one_row = at.send(swap_row, one)
        other_fed = feed(
            False,
            "feed",
            [quads(m_next, m_next_row), quads(m_far, m_far_row), quads(m_both, m_both_row)],
            [quads(t_next, t_next_row), quads(t_far, t_far_row), quads(t_both, t_both_row)],
            shared,
            hidden_layer,
            at.before,
        )
        mlp_terms = [
            term(fed.top, other_fed.top, fed.hidden, other_fed.hidden),
            term(fed.normed, other_fed.normed, fed.gi, other_fed.gi),
            term(fed.normed, other_fed.normed, fed.gl, other_fed.gl),
        ]
        mlp_sent = product("mlp_partial", mlp_terms, low ^ SIDE, at.before)
        at.ran(mlp_sent[0])
        at.end()
        one = one + one_row

        value_came.append(at.send(following, value_sent[1]))
        mlp_came = [at.send(side, mlp_sent[0])]
        one_core = at.send(swap_core, one)
        ff_row = at.send(swap_row, ff)
        value_mine = product("value_mine", value_terms, low, at.before)
        key_mine = product("key_mine", key_terms, low, at.before)
        mlp_mine = product("mlp_mine", mlp_terms, low, at.before)
        at.ran(value_mine[0], key_mine[0], mlp_mine[0])
        at.end()
        ff = middle + (ff + ff_row)

        value_came.append(at.send(following, value_sent[2]))
        mlp_came.append(at.send(side, mlp_sent[1]))
        ff_core = at.send(swap_core, ff)
        finish = input_gradient(
            [one, one_core],
            inputs,
            grad.grad,
            info,
            shared.first_gain,
            at.before,
        )
        at.ran(finish.out)
        at.end()

        mlp_came.append(at.send(side, mlp_sent[2]))
        key_came.append(at.send(following, key_sent[1]))
        outputs = joined([ff, ff_core], info, width, at.before)
        grad_down, grad_inner, grad_linear = map(finished, mlp_mine, mlp_came)
        grad_out, grad_gate, grad_value = map(finished, value_mine, value_came)
        grad_query, grad_key = [finished(a, b, 0) for a, b in zip(key_mine, key_came)]

        sums = jnp.concatenate(
            [
                grad.gain_sum[0],
                grad.bias_sum[0],
                finish.gain_sum[0],
                finish.bias_sum[0],
                backed.head_sum[:, 0],
            ]
        )
        bit = dp // 2
        while bit:
            sums = sums + swap_dp(gate(sums, at.before), bit)
            bit //= 2
        vector = lambda i: sums[i * width : (i + 1) * width]
        return (
            outputs,
            finish.out,
            grad_query,
            grad_key,
            grad_value.T,
            grad_gate.T,
            grad_out,
            grad_inner.T,
            grad_linear.T,
            grad_down,
            vector(2),
            vector(3),
            sums[4 * width :],
            vector(0),
            vector(1),
        )

    return body


def solution(mesh):
    in_specs = (
        P("dp", None),
        P("dp"),
        P(None, "tensor"),
        P(None, "tensor"),
        P(None, "tensor"),
        P(None, "tensor"),
        P("tensor", None),
        P(None, "tensor"),
        P(None, "tensor"),
        P("tensor", None),
        P(),
        P(),
        P("tensor"),
        P(),
        P(),
        P("dp", None),
    )
    out_specs = (
        P("dp", None),
        P("dp", None),
        P("dp", "tensor"),
        P("dp", "tensor"),
        P("dp", "tensor"),
        P("dp", "tensor"),
        P("tensor", "dp"),
        P("dp", "tensor"),
        P("dp", "tensor"),
        P("tensor", "dp"),
        P(),
        P(),
        P("tensor"),
        P(),
        P(),
    )
    body = make_body(mesh.shape["dp"], mesh.shape["tensor"])
    return jax.shard_map(body, mesh=mesh, in_specs=in_specs, out_specs=out_specs, check_vma=False)
```

```python
import functools
from types import SimpleNamespace

import jax
import jax.numpy as jnp
from jax import lax
from jax.experimental import pallas as pl
from jax.experimental.pallas import tpu as pltpu
from jax.sharding import PartitionSpec as P

KD = 256
VD = 432
DOCS_DEV = 8
SIDE = 1
NEXT = 2
FAR = 4
BITS = 8

EPS = 1e-05
HEAD_EPS = 0.25
SCALE = KD ** (-0.5)

F32 = jnp.float32
BF16 = jnp.bfloat16
AXES = ("dp", "tensor")


def dot(a, b, ca, cb):
    return lax.dot_general(a, b, (((ca,), (cb,)), ((), ())), preferred_element_type=F32)


def nn(a, b):
    return dot(a, b, 1, 0)


def nt(a, b):
    return dot(a, b, 1, 1)


def tn(a, b):
    return dot(a, b, 0, 0)


def standard(value, epsilon, axis):
    center = value - jnp.mean(value, axis, keepdims=True)
    inverse = lax.rsqrt(jnp.mean(center * center, axis, keepdims=True) + epsilon)
    return center * inverse, inverse


def norm_back(upstream, unit, inverse, gain, axis):
    scaled = upstream * gain
    return inverse * (
        scaled
        - jnp.mean(scaled, axis, keepdims=True)
        - unit * jnp.mean(scaled * unit, axis, keepdims=True)
    )


class Call:
    def __init__(self, blocks, rows=None):
        self.blocks, self.rows = blocks, rows
        self.keys, self.arrays, self.specs = [], [], []
        self.out_keys, self.outs, self.out_specs = [], [], []
        self.temp_keys, self.temps = [], []

    def add(self, key, array, spec):
        self.keys.append(key)
        self.arrays.append(array)
        self.specs.append(spec)

    def spec(self, shape, **mode):
        if self.rows and shape[0] == self.rows:
            return pl.BlockSpec((self.rows // self.blocks, shape[1]), lambda b: (b, 0))
        return pl.BlockSpec(shape, zeros(len(shape)), **mode)

    def whole(self, **arrays):
        for key, array in arrays.items():
            self.add(key, array, self.spec(array.shape, pipeline_mode=pl.Buffered(1)))

    def scalars(self, **arrays):
        for key, array in arrays.items():
            self.add(key, array, pl.BlockSpec(memory_space=pltpu.SMEM))

    def cut(self, **arrays):
        for key, array in arrays.items():
            self.add(key, array, leading(array.shape[1:]))

    def pieces(self, **groups):
        for key, group in groups.items():
            for block, runs in enumerate(group):
                for run, parts in enumerate(runs):
                    for part in parts:
                        spec = self.spec(part.shape, pipeline_mode=pl.Buffered(1))
                        self.add((key, block, run), part, spec)

    def after(self, *arrays):
        for array in arrays:
            self.add(None, array, pl.BlockSpec(memory_space=pl.ANY))

    def result(self, **forms):
        for key, (shape, dtype) in forms.items():
            self.out_keys.append(key)
            self.outs.append(jax.ShapeDtypeStruct(shape, dtype))
            self.out_specs.append(self.spec(shape))

    def results(self, **forms):
        for key, (shape, dtype) in forms.items():
            self.out_keys.append(key)
            self.outs.append(jax.ShapeDtypeStruct((self.blocks,) + shape, dtype))
            self.out_specs.append(leading(shape))

    def temp(self, **forms):
        for key, (shape, dtype) in forms.items():
            self.temp_keys.append(key)
            self.temps.append(pltpu.VMEM(shape, dtype))

    def run(self, name, body):
        keys = self.keys + self.out_keys + self.temp_keys

        def kernel(*refs):
            r = SimpleNamespace()
            for key, ref in zip(keys, refs):
                if isinstance(key, tuple):
                    runs = r.__dict__.setdefault(key[0], {}).setdefault(key[1], {})
                    runs.setdefault(key[2], []).append(ref)
                elif key is not None:
                    setattr(r, key, ref)
            body(r)

        got = pl.pallas_call(
            kernel,
            grid=(self.blocks,),
            in_specs=self.specs,
            out_specs=self.out_specs,
            out_shape=self.outs,
            scratch_shapes=self.temps,
            cost_estimate=LIGHT,
            name=name,
        )(*self.arrays)
        return SimpleNamespace(**dict(zip(self.out_keys, got)))


LIGHT = pl.CostEstimate(flops=1, transcendentals=0, bytes_accessed=1)


def zeros(n):
    return lambda *g: (0,) * n


def leading(shape):
    rest = (0,) * len(shape)
    return pl.BlockSpec((None,) + shape, lambda b: (b,) + rest)


STEP = 32


def by_rows(rows, step, run):
    @pl.loop(0, rows // step)
    def _(i):
        run(pl.ds(pl.multiple_of(i * step, step), step))


def place_pieces(r, target, group, width):
    core = r.info[0]
    row = r.info[1]

    def put(runs):
        first = 0
        for parts in runs.values():
            size = width // len(parts)
            if len(parts) == 4:
                far = (1 - core) * 2
                at = [core * 2 + row, core * 2 + 1 - row, far + row, far + 1 - row]
            else:
                at = [core, 1 - core]
            cuts = [pl.ds(pl.multiple_of(a * size, size), size) for a in at]

            def move(here, start=first):
                for part, cut in zip(parts, cuts):
                    there = pl.ds(pl.multiple_of(start + here.start, STEP), STEP)
                    target[there, cut] = part[here, :]

            by_rows(parts[0].shape[0], STEP, move)
            first += parts[0].shape[0]

    if len(group) == 1:
        put(group[0])
    else:
        for block, runs in group.items():
            pl.when(pl.program_id(0) == block)(functools.partial(put, runs))


def downwards(r):
    across = r.document[...].astype(F32)
    rows = across.shape[1]
    return jnp.broadcast_to(across, (rows, rows)).T


def decays(r, heads):
    down = downwards(r)
    rows = down.shape[0]
    n = lax.broadcasted_iota(jnp.int32, (rows, rows), 0)
    m = lax.broadcasted_iota(jnp.int32, (rows, rows), 1)
    allowed = (n >= m) & (down == r.document[...].astype(F32))
    spread = jnp.where(allowed, (n - m).astype(F32), 0.0)
    return [jnp.where(allowed, jnp.exp(spread * r.rates[h]), 0.0) for h in range(heads)]


def half_columns(r, width):
    size = width // 2
    return [pl.ds(pl.multiple_of(a * size, size), size) for a in (r.info[0], 1 - r.info[0])]


def attend(own, name, source, document, shared, weights, heads, after=()):
    query_w, key_w, value_wt, gate_wt, out_w = weights
    blocks, unused, rows = document.shape
    width = query_w.shape[0]
    features = value_wt.shape[0]
    c = Call(blocks)
    c.scalars(info=shared.info, rates=shared.rates)
    c.whole(gain=shared.first_gain, bias=shared.first_bias, head_gain=shared.head_gain)
    c.cut(document=document)
    c.whole(qw=query_w, kw=key_w, vw=value_wt, gw=gate_wt)
    c.after(*after)
    if own:
        c.whole(x=source, ow=out_w)
        part = ((rows, width // 2), F32)
        c.result(near=part, away=part)
    else:
        c.pieces(x=source)
        c.temp(x_rows=((rows, width), F32))
    wide = ((rows, heads * KD), BF16)
    tall = ((features, rows), BF16)
    tall_f = ((features, rows), F32)
    c.results(
        normed=((rows, width), BF16),
        q=wide,
        k=wide,
        v=tall,
        s=((heads, rows, rows), BF16),
        g=tall_f,
        hat=tall_f,
        inv=((heads, 1, rows), F32),
        gated=tall,
    )

    def body(r):
        if own:
            x = r.x[...].astype(F32)
        else:
            place_pieces(r, r.x_rows, r.x, width)
            x = r.x_rows[...]
        hat, unused = standard(x, EPS, 1)
        normed = (hat * r.gain[...] + r.bias[...]).astype(BF16)
        r.normed[...] = normed
        r.q[...] = nn(normed, r.qw[...]).astype(BF16)
        r.k[...] = (nn(normed, r.kw[...]) * SCALE).astype(BF16)
        r.v[...] = nt(r.vw[...], normed).astype(BF16)
        r.g[...] = nt(r.gw[...], normed)
        decay = decays(r, heads)
        for h in range(heads):
            kd = pl.ds(h * KD, KD)
            vd = pl.ds(h * VD, VD)
            score = (nt(r.q[:, kd], r.k[:, kd]) * decay[h]).astype(BF16)
            r.s[h] = score
            head_hat, head_inv = standard(nt(r.v[vd, :], score), HEAD_EPS, 0)
            r.hat[vd, :] = head_hat
            r.inv[h] = head_inv
            gates = r.g[vd, :]
            swish = gates * jax.nn.sigmoid(gates)
            r.gated[vd, :] = (swish * (head_hat * r.head_gain[vd, :])).astype(BF16)
        if own:
            for cut, out in zip(half_columns(r, width), (r.near, r.away)):
                out[...] = tn(r.gated[...], r.ow[:, cut])

    return c.run(name, body)


def feed(own, name, middle, top, shared, weights, after=()):
    inner_wt, linear_wt, down_w = weights
    features, width = inner_wt.shape
    blocks, rows = len(middle), shared.rows
    c = Call(blocks)
    c.scalars(info=shared.info)
    c.whole(gain=shared.second_gain, bias=shared.second_bias)
    c.pieces(m=middle)
    c.whole(iw=inner_wt, lw=linear_wt, dw=down_w)
    c.after(*after)
    c.temp(m_rows=((rows, width), F32))
    if own:
        c.whole(c=top)
        part = ((rows, width // 2), F32)
        c.result(two_near=part, two_away=part, ff_near=part, ff_away=part)
    else:
        c.pieces(c=top)
        c.temp(c_rows=((rows, width), F32))
    flat = ((rows, width), BF16)
    tall = ((features, rows), BF16)
    c.results(normed=flat, top=flat, hidden=tall, gi=tall, gl=tall)

    def body(r):
        place_pieces(r, r.m_rows, r.m, width)
        hat, unused = standard(r.m_rows[...], EPS, 1)
        r.normed[...] = (hat * r.gain[...] + r.bias[...]).astype(BF16)
        if own:
            r.top[...] = r.c[...]
        else:
            place_pieces(r, r.c_rows, r.c, width)
            r.top[...] = r.c_rows[...].astype(BF16)
        for at in range(0, features, VD):
            cut = pl.ds(at, VD)
            inner = nt(r.iw[cut, :], r.normed[...])
            linear = nt(r.lw[cut, :], r.normed[...])
            upstream = nt(r.dw[cut, :], r.top[...])
            cumulative = 0.5 * (1.0 + lax.erf(inner * 0.7071067811865476))
            gelu = inner * cumulative
            slope = cumulative + inner * jnp.exp(-0.5 * inner * inner) * 0.3989422804014327
            r.hidden[cut, :] = (gelu * linear).astype(BF16)
            r.gi[cut, :] = (upstream * linear * slope).astype(BF16)
            r.gl[cut, :] = (upstream * gelu).astype(BF16)
        if own:
            cuts = half_columns(r, width)
            for cut, out in zip(cuts, (r.two_near, r.two_away)):
                out[...] = tn(r.gi[...], r.iw[:, cut]) + tn(r.gl[...], r.lw[:, cut])
            for cut, out in zip(cuts, (r.ff_near, r.ff_away)):
                out[...] = tn(r.hidden[...], r.dw[:, cut])

    return c.run(name, body)


def add_sums(r, upstream, hat):
    @pl.when(pl.program_id(0) == 0)
    def _():
        r.gain_sum[...] = jnp.zeros(r.gain_sum.shape, F32)
        r.bias_sum[...] = jnp.zeros(r.bias_sum.shape, F32)

    r.gain_sum[...] += jnp.sum(upstream * hat, 0, keepdims=True)
    r.bias_sum[...] += jnp.sum(upstream, 0, keepdims=True)


def middle_back(middle, upstream, top, shared, after=()):
    rows, width = top.shape
    c = Call(4, rows)
    c.scalars(info=shared.info)
    c.whole(gain=shared.second_gain, top=top)
    c.pieces(m=middle, u=upstream)
    c.after(*after)
    flat = ((rows, width), F32)
    line = ((1, width), F32)
    part = ((rows // 4, width), F32)
    c.temp(m_rows=part, u_rows=part)
    c.result(grad=flat, half=((rows, width // 2), F32), gain_sum=line, bias_sum=line)
    c.result(quarter=((rows, width // 4), F32))

    def body(r):
        place_pieces(r, r.m_rows, r.m, width)
        place_pieces(r, r.u_rows, r.u, width)
        hat, inverse = standard(r.m_rows[...], EPS, 1)
        upstream = r.u_rows[...]
        add_sums(r, upstream, hat)
        r.grad[...] = r.top[...].astype(F32) + norm_back(
            upstream, hat, inverse, r.gain[...], 1
        )
        r.half[...] = r.grad[:, half_columns(r, width)[0]]
        n = width // 4
        at = (r.info[0] * 2 + r.info[1]) * n
        r.quarter[...] = r.grad[:, pl.ds(pl.multiple_of(at, n), n)]

    return c.run("middle_back", body)


def back(own, name, grad, state, document, shared, weights, heads, after=()):
    query_w, key_w, value_wt, gate_wt, out_w = weights
    width = query_w.shape[0]
    features = value_wt.shape[0]
    blocks, unused, rows = document.shape
    c = Call(blocks)
    c.scalars(info=shared.info, rates=shared.rates)
    c.whole(head_gain=shared.head_gain)
    c.cut(document=document)
    c.cut(q=state.q, k=state.k, v=state.v, s=state.s, g=state.g, hat=state.hat, inv=state.inv)
    c.whole(ow=out_w)
    c.after(*after)
    if own:
        c.whole(m=grad, qw=query_w, kw=key_w, vw=value_wt, gw=gate_wt)
        part = ((rows, width // 2), F32)
        c.result(near=part, away=part, head_sum=((features, 1), F32))
    else:
        c.pieces(m=grad)
        c.temp(m_rows=((rows, width), F32))
    wide = ((rows, heads * KD), BF16)
    tall = ((features, rows), BF16)
    c.results(gm=((rows, width), BF16), gq=wide, gk=wide, gv=tall, gg=tall)

    def body(r):
        if own:
            r.gm[...] = r.m[...].astype(BF16)
        else:
            place_pieces(r, r.m_rows, r.m, width)
            r.gm[...] = r.m_rows[...].astype(BF16)
        decay = decays(r, heads)
        for h in range(heads):
            kd = pl.ds(h * KD, KD)
            vd = pl.ds(h * VD, VD)
            grad_gated = nt(r.ow[vd, :], r.gm[...])
            gates = r.g[vd, :]
            head_hat = r.hat[vd, :]
            gain = r.head_gain[vd, :]
            sigma = jax.nn.sigmoid(gates)
            r.gg[vd, :] = (
                grad_gated * (head_hat * gain) * sigma * (1.0 + gates * (1.0 - sigma))
            ).astype(BF16)
            grad_normed = grad_gated * (gates * sigma)
            if own:
                r.head_sum[vd, :] = jnp.sum(grad_normed * head_hat, 1, keepdims=True)
            mixed = norm_back(grad_normed, head_hat, r.inv[h], gain, 0).astype(BF16)
            masked = (tn(mixed, r.v[vd, :]) * decay[h]).astype(BF16)
            r.gv[vd, :] = nn(mixed, r.s[h]).astype(BF16)
            r.gq[:, kd] = nn(masked, r.k[:, kd]).astype(BF16)
            r.gk[:, kd] = (tn(masked, r.q[:, kd]) * SCALE).astype(BF16)
        if own:
            for cut, out in zip(half_columns(r, width), (r.near, r.away)):
                out[...] = (
                    nt(r.gq[...], r.qw[cut, :])
                    + nt(r.gk[...], r.kw[cut, :])
                    + tn(r.gv[...], r.vw[:, cut])
                    + tn(r.gg[...], r.gw[:, cut])
                )

    return c.run(name, body)


def weigh(name, terms, which, after=()):
    arrays, specs, outs, out_specs = [], [], [], []
    ends = []
    for array in terms[0][0]:
        ends.append(array.shape[0] + (ends[-1] if ends else 0))

    def at(i, b):
        count = terms[0][0][i].shape[0]
        return jnp.clip(b - (ends[i] - count), 0, count - 1) if count > 1 else 0

    for lefts, rights, turned, size in terms:
        for i, left in enumerate(lefts):
            arrays.append(left)
            specs.append(
                pl.BlockSpec((None, left.shape[1], size), lambda b, w, i=i: (at(i, b), 0, w[0]))
            )
        for i, right in enumerate(rights):
            arrays.append(right)
            specs.append(
                pl.BlockSpec((None,) + right.shape[1:], lambda b, w, i=i: (at(i, b), 0, 0))
            )
        shape = (size, right.shape[2]) if turned else (right.shape[1], size)
        outs.append(jax.ShapeDtypeStruct(shape, F32))
        out_specs.append(pl.BlockSpec(shape, lambda b, w: (0, 0)))
    for array in after:
        arrays.append(array)
        specs.append(pl.BlockSpec(memory_space=pl.ANY))
    n = len(ends)

    def kernel(w, *refs):
        results = refs[len(arrays) :]
        b = pl.program_id(0)

        def pick(some):
            value = some[-1][...]
            for end, ref in zip(ends[-2::-1], some[-2::-1]):
                value = lax.select(b < end, ref[...], value)
            return value

        for i, result in enumerate(results):
            left = pick(refs[2 * n * i : 2 * n * i + n])
            right = pick(refs[2 * n * i + n : 2 * n * i + 2 * n])
            got = tn(left, right) if terms[i][2] else nn(right, left)
            result[...] = lax.select(b > 0, result[...], jnp.zeros_like(got)) + got

    return pl.pallas_call(
        kernel,
        grid_spec=pltpu.PrefetchScalarGridSpec(
            num_scalar_prefetch=1, grid=(ends[-1],), in_specs=specs, out_specs=out_specs
        ),
        out_shape=outs,
        cost_estimate=LIGHT,
        name=name,
    )(which, *arrays)


def joined(pieces, info, width, after=()):
    rows = pieces[0].shape[0]
    c = Call(4, rows)
    c.scalars(info=info)
    c.pieces(y=[[pieces]])
    c.after(*after)
    c.result(out=((rows, width), F32))
    return c.run("joined", lambda r: place_pieces(r, r.out, r.y, width)).out


def input_gradient(pieces, inputs, middle, info, gain, after=()):
    rows, width = inputs.shape
    c = Call(4, rows)
    c.scalars(info=info)
    c.whole(gain=gain, x=inputs, middle=middle)
    c.pieces(u=[[pieces]])
    c.after(*after)
    line = ((1, width), F32)
    c.result(out=((rows, width), F32), gain_sum=line, bias_sum=line)
    c.temp(u_rows=((rows // 4, width), F32))

    def body(r):
        place_pieces(r, r.u_rows, r.u, width)
        hat, inverse = standard(r.x[...].astype(F32), EPS, 1)
        upstream = r.u_rows[...]
        add_sums(r, upstream, hat)
        r.out[...] = r.middle[...] + norm_back(upstream, hat, inverse, r.gain[...], 1)

    return c.run("finish", body)


def make_body(dp, tp):
    hi_count = dp // BITS

    def permute(x, target):
        pairs = []
        for d in range(dp):
            for t in range(tp):
                to_d, to_t = target(d, t)
                pairs.append((d * tp + t, to_d * tp + to_t))
        return lax.ppermute(x, AXES, pairs)

    swap_core = lambda x: permute(x, lambda d, t: (d, t ^ 1))
    swap_row = lambda x: permute(x, lambda d, t: (d, t ^ 2))
    swap_dp = lambda x, bit: permute(x, lambda d, t: (d ^ bit, t))

    gate = lambda x, earlier: lax.optimization_barrier((x,) + tuple(earlier))[0] if earlier else x

    class Stages:
        def __init__(self):
            self.before, self.now, self.sends = [], [], 0
            self.spare, self.fresh = [], []

        def send(self, swap, x, free=False):
            got = swap(x if free else gate(x, self.before))
            self.now.append(got)
            self.sends += 1
            return got

        def ran(self, *arrays):
            self.now += arrays

        def later(self, x):
            slot = [x, None]
            self.fresh.append(slot)
            return slot

        def end(self, limit=5):
            while self.spare and self.sends < limit:
                slot = self.spare.pop(0)
                slot[1] = self.send(swap_core, slot[0])
            self.spare, self.fresh = self.spare + self.fresh, []
            self.before, self.now, self.sends = self.now, [], 0

    def body(
        inputs,
        document,
        query_weight,
        key_weight,
        value_weight,
        gate_weight,
        out_weight,
        inner_weight,
        linear_weight,
        down_weight,
        first_gain,
        first_bias,
        head_gain,
        second_gain,
        second_bias,
        cotangent,
    ):
        rows, width = inputs.shape
        share = width // dp
        heads = query_weight.shape[1] // KD
        d = lax.axis_index("dp")
        t = lax.axis_index("tensor")
        core = t % 2
        row = t // 2
        info = jnp.stack([core, row]).astype(jnp.int32)
        numbers = (t * heads + jnp.arange(heads)).astype(F32)
        shared = SimpleNamespace(
            info=info,
            rows=rows,
            rates=jnp.log1p(-jnp.exp2(-5.0 - numbers)),
            first_gain=first_gain[None],
            first_bias=first_bias[None],
            second_gain=second_gain[None],
            second_bias=second_bias[None],
            head_gain=head_gain[:, None],
        )
        attention = (query_weight, key_weight, value_weight.T, gate_weight.T, out_weight)
        hidden_layer = (inner_weight.T, linear_weight.T, down_weight)

        low = d % BITS

        def share_of(x, place):
            cuts = [
                lax.dynamic_slice_in_dim(x, (hi * BITS + place) * share, share, x.ndim - 1)
                for hi in range(hi_count)
            ]
            return jnp.concatenate(cuts, x.ndim - 1)

        def over_hi(x, axis):
            hi = d // BITS
            cut = lambda k: lax.dynamic_slice_in_dim(x, (hi ^ k) * share, share, axis)
            total = cut(0)
            for k in range(1, hi_count):
                total = total + swap_dp(cut(k), k * BITS)
            return total

        def product(name, terms, place, after=()):
            ready = []
            for lefts, rights, turned in terms:
                if hi_count > 1:
                    lefts = [share_of(left, place) for left in lefts]
                ready.append((lefts, rights, turned, hi_count * share))
            index = place if hi_count == 1 else place * 0
            return weigh(name, ready, index.reshape(1).astype(jnp.int32), after)

        def finished(mine, arrived, axis=1):
            total = gate(mine, at.before) + arrived
            return over_hi(total, axis) if hi_count > 1 else total

        def term(lefts, rights, turned=False):
            return (lefts, rights, turned)

        side = lambda x: swap_dp(x, SIDE)
        following = lambda x: swap_dp(x, NEXT)
        far = lambda x: swap_dp(x, FAR)
        stack = lambda *parts: jnp.concatenate(parts, 0)

        def half(array):
            return lax.dynamic_slice_in_dim(array, core * (width // 2), width // 2, 1).astype(F32)

        def quarter(halved):
            return lax.dynamic_slice_in_dim(halved, row * (width // 4), width // 4, 1)

        def pairs(*slots):
            return [[slot[0], slot[1]] for slot in slots]

        def quads(one, two):
            return [[one[0], two[0], one[1], two[1]]]

        own_doc = document[None, None]
        live = (document < DOCS_DEV)[:, None]
        top = jnp.where(live, cotangent, jnp.zeros((), BF16))
        top_quarter = quarter(half(top))
        input_half = half(inputs)
        k = rows // 4
        at = Stages()

        doc_side = at.send(side, document)
        doc_far = at.send(far, document)
        x_side = [at.later(at.send(side, input_half[: 2 * k]))]
        t_next = at.later(at.send(following, top_quarter))
        x_far = [None, at.later(at.send(far, input_half[2 * k : 3 * k]))]
        own = attend(True, "attend_own", inputs, own_doc, shared, attention, heads)
        at.ran(own.near)
        at.end(0)

        branch = own.near + at.send(swap_core, own.away)
        at.end(2)

        branch_row = at.send(swap_row, branch)
        doc_both = at.send(side, doc_far)
        x_side.append(at.later(at.send(side, input_half[2 * k :])))
        x_far[0] = at.later(at.send(far, input_half[: 2 * k]))
        at.end()
        middle = input_half + (branch + branch_row)

        middle_core = at.send(swap_core, middle)
        at.end(3)

        x_far.append(at.later(at.send(far, input_half[3 * k :])))
        x_both = [at.later(at.send(side, x_far[0][0]))]
        t_next_row = at.later(at.send(swap_row, t_next[0]))
        middle_own = [[[middle, middle_core]]]
        fed = feed(True, "feed_own", middle_own, top, shared, hidden_layer, at.before)
        at.ran(fed.two_near)
        at.end()

        two = fed.two_near + at.send(swap_core, fed.two_away)
        at.end(2)

        two_row = at.send(swap_row, two)
        m_next = at.later(at.send(following, quarter(middle)))
        m_far = at.later(at.send(far, quarter(middle)))
        x_both.append(at.later(at.send(side, stack(x_far[1][0], x_far[2][0]))))
        ff = fed.ff_near + at.send(swap_core, fed.ff_away)
        at.ran(ff)
        at.end()
        two = two + two_row

        two_core = at.send(swap_core, two)
        at.end(4)

        grad = middle_back(middle_own, [[[two, two_core]]], top, shared, at.before)
        at.ran(grad.grad)
        at.end(9)

        g_side = at.send(side, grad.half)
        g_far = at.send(far, grad.quarter)
        m_next_row = at.send(swap_row, m_next[0])
        m_far_row = at.send(swap_row, m_far[0])
        m_next_row, g_side, g_far, m_far_row = map(
            at.later, (m_next_row, g_side, g_far, m_far_row)
        )
        other_doc = jnp.stack([doc_side, doc_far, doc_both])[:, None]
        others = attend(
            False,
            "attend",
            [pairs(*x_side), pairs(*x_far), pairs(*x_both)],
            other_doc,
            shared,
            attention,
            heads,
            at.before,
        )
        at.ran(others.q)
        at.end()

        g_both = at.later(at.send(side, g_far[0]))
        g_far_row = at.later(at.send(swap_row, g_far[0]))
        m_both = at.later(at.send(following, m_far[0]))
        t_far = at.send(far, top_quarter[: 2 * k])
        backed = back(
            True, "back_own", grad.grad, own, own_doc, shared, attention, heads, at.before
        )
        at.ran(backed.near)
        at.end()

        g_both_row = at.send(swap_row, g_both[0])
        t_far = stack(t_far, at.send(far, top_quarter[2 * k :]))
        one = backed.near + at.send(swap_core, backed.away)
        first_fed = feed(
            False,
            "feed_next",
            [quads(m_next, m_next_row)],
            [quads(t_next, t_next_row)],
            shared,
            hidden_layer,
            at.before,
        )
        at.ran(first_fed.gi)
        at.end()
        t_far = at.later(t_far)

        g_both_row = [g_both_row, at.send(swap_core, g_both_row)]
        at.end(5)

        t_both = at.later(at.send(following, t_far[0]))
        m_both_row = at.later(at.send(swap_row, m_both[0]))
        t_far_row = at.later(at.send(swap_row, t_far[0]))
        other_backed = back(
            False,
            "back",
            [pairs(g_side), quads(g_far, g_far_row), quads(g_both, g_both_row)],
            others,
            other_doc,
            shared,
            attention,
            heads,
            at.before,
        )
        first_normed = [own.normed, others.normed]
        value_terms = [
            term([backed.gm, other_backed.gm], [own.gated, others.gated]),
            term(first_normed, [backed.gg, other_backed.gg]),
            term(first_normed, [backed.gv, other_backed.gv]),
        ]
        key_terms = [
            term(first_normed, [backed.gq, other_backed.gq], True),
            term(first_normed, [backed.gk, other_backed.gk], True),
        ]
        key_sent = product("key_partial", key_terms, low ^ NEXT, at.before)
        at.ran(other_backed.gq, key_sent[0])
        at.end()

        t_both_row = at.send(swap_row, t_both[0])
        key_came = [at.send(following, key_sent[0])]
        value_sent = product("value_partial", value_terms, low ^ NEXT, at.before)
        at.ran(value_sent[0], one)
        at.end(6)

        t_both_row = [t_both_row, at.send(swap_core, t_both_row)]
        at.end(4)

        value_came = [at.send(following, value_sent[0])]
        one_row = at.send(swap_row, one)
        other_fed = feed(
            False,
            "feed",
            [quads(m_far, m_far_row), quads(m_both, m_both_row)],
            [quads(t_far, t_far_row), quads(t_both, t_both_row)],
            shared,
            hidden_layer,
            at.before,
        )
        feds = [fed, first_fed, other_fed]
        second_normed = [f.normed for f in feds]
        mlp_terms = [
            term([f.top for f in feds], [f.hidden for f in feds]),
            term(second_normed, [f.gi for f in feds]),
            term(second_normed, [f.gl for f in feds]),
        ]
        mlp_sent = product("mlp_partial", mlp_terms, low ^ SIDE, at.before)
        at.ran(mlp_sent[0])
        at.end()
        one = one + one_row

        value_came.append(at.send(following, value_sent[1]))
        mlp_came = [at.send(side, mlp_sent[0])]
        one_core = at.send(swap_core, one)
        ff_row = at.send(swap_row, ff)
        value_mine = product("value_mine", value_terms, low, at.before)
        key_mine = product("key_mine", key_terms, low, at.before)
        mlp_mine = product("mlp_mine", mlp_terms, low, at.before)
        at.ran(value_mine[0], key_mine[0], mlp_mine[0])
        at.end()
        ff = middle + (ff + ff_row)

        value_came.append(at.send(following, value_sent[2]))
        mlp_came.append(at.send(side, mlp_sent[1]))
        ff_core = at.send(swap_core, ff)
        finish = input_gradient(
            [one, one_core],
            inputs,
            grad.grad,
            info,
            shared.first_gain,
            at.before,
        )
        sums = jnp.concatenate(
            [
                grad.gain_sum[0],
                grad.bias_sum[0],
                finish.gain_sum[0],
                finish.bias_sum[0],
                backed.head_sum[:, 0],
            ]
        )
        sums = sums + at.send(side, sums, free=True)
        at.ran(finish.out)
        at.end()

        mlp_came.append(at.send(side, mlp_sent[2]))
        key_came.append(at.send(following, key_sent[1]))
        outputs = joined([ff, ff_core], info, width, at.before)
        grad_down, grad_inner, grad_linear = map(finished, mlp_mine, mlp_came)
        grad_out, grad_gate, grad_value = map(finished, value_mine, value_came)
        grad_query, grad_key = [finished(a, b, 0) for a, b in zip(key_mine, key_came)]

        ready = (key_came[1], outputs, grad_down, grad_inner, grad_out, grad_gate, grad_value)
        sums_next, sums_far, sums_both = [
            swap_dp(gate(sums, ready), bit) for bit in (NEXT, FAR, NEXT | FAR)
        ]
        sums = (sums + sums_next) + (sums_far + sums_both)
        bit = BITS
        while bit < dp:
            sums = sums + swap_dp(sums, bit)
            bit *= 2
        vector = lambda i: sums[i * width : (i + 1) * width]
        return (
            outputs,
            finish.out,
            grad_query,
            grad_key,
            grad_value.T,
            grad_gate.T,
            grad_out,
            grad_inner.T,
            grad_linear.T,
            grad_down,
            vector(2),
            vector(3),
            sums[4 * width :],
            vector(0),
            vector(1),
        )

    return body


def solution(mesh):
    in_specs = (
        P("dp", None),
        P("dp"),
        P(None, "tensor"),
        P(None, "tensor"),
        P(None, "tensor"),
        P(None, "tensor"),
        P("tensor", None),
        P(None, "tensor"),
        P(None, "tensor"),
        P("tensor", None),
        P(),
        P(),
        P("tensor"),
        P(),
        P(),
        P("dp", None),
    )
    out_specs = (
        P("dp", None),
        P("dp", None),
        P("dp", "tensor"),
        P("dp", "tensor"),
        P("dp", "tensor"),
        P("dp", "tensor"),
        P("tensor", "dp"),
        P("dp", "tensor"),
        P("dp", "tensor"),
        P("tensor", "dp"),
        P(),
        P(),
        P("tensor"),
        P(),
        P(),
    )
    body = make_body(mesh.shape["dp"], mesh.shape["tensor"])
    return jax.shard_map(body, mesh=mesh, in_specs=in_specs, out_specs=out_specs, check_vma=False)
```

```python
import functools
from types import SimpleNamespace

import jax
import jax.numpy as jnp
from jax import lax
from jax.experimental import pallas as pl
from jax.experimental.pallas import tpu as pltpu
from jax.sharding import PartitionSpec as P

KD = 256
VD = 432
DOCS_DEV = 8
SIDE = 1
NEXT = 2
FAR = 4
BITS = 8

EPS = 1e-05
HEAD_EPS = 0.25
SCALE = KD ** (-0.5)

F32 = jnp.float32
BF16 = jnp.bfloat16
AXES = ("dp", "tensor")


def dot(a, b, ca, cb):
    return lax.dot_general(a, b, (((ca,), (cb,)), ((), ())), preferred_element_type=F32)


def nn(a, b):
    return dot(a, b, 1, 0)


def nt(a, b):
    return dot(a, b, 1, 1)


def tn(a, b):
    return dot(a, b, 0, 0)


def standard(value, epsilon, axis):
    center = value - jnp.mean(value, axis, keepdims=True)
    inverse = lax.rsqrt(jnp.mean(center * center, axis, keepdims=True) + epsilon)
    return center * inverse, inverse


def norm_back(upstream, unit, inverse, gain, axis):
    scaled = upstream * gain
    return inverse * (
        scaled
        - jnp.mean(scaled, axis, keepdims=True)
        - unit * jnp.mean(scaled * unit, axis, keepdims=True)
    )


class Call:
    def __init__(self, blocks, rows=None):
        self.blocks, self.rows = blocks, rows
        self.keys, self.arrays, self.specs = [], [], []
        self.out_keys, self.outs, self.out_specs = [], [], []
        self.temp_keys, self.temps = [], []

    def add(self, key, array, spec):
        self.keys.append(key)
        self.arrays.append(array)
        self.specs.append(spec)

    def spec(self, shape, **mode):
        if self.rows and shape[0] == self.rows:
            return pl.BlockSpec((self.rows // self.blocks, shape[1]), lambda b: (b, 0))
        return pl.BlockSpec(shape, zeros(len(shape)), **mode)

    def whole(self, **arrays):
        for key, array in arrays.items():
            self.add(key, array, self.spec(array.shape, pipeline_mode=pl.Buffered(1)))

    def scalars(self, **arrays):
        for key, array in arrays.items():
            self.add(key, array, pl.BlockSpec(memory_space=pltpu.SMEM))

    def cut(self, **arrays):
        for key, array in arrays.items():
            self.add(key, array, leading(array.shape[1:]))

    def pieces(self, **groups):
        for key, group in groups.items():
            for block, runs in enumerate(group):
                for run, parts in enumerate(runs):
                    for part in parts:
                        spec = self.spec(part.shape, pipeline_mode=pl.Buffered(1))
                        self.add((key, block, run), part, spec)

    def after(self, *arrays):
        for array in arrays:
            self.add(None, array, pl.BlockSpec(memory_space=pl.ANY))

    def result(self, **forms):
        for key, (shape, dtype) in forms.items():
            self.out_keys.append(key)
            self.outs.append(jax.ShapeDtypeStruct(shape, dtype))
            self.out_specs.append(self.spec(shape))

    def results(self, **forms):
        for key, (shape, dtype) in forms.items():
            self.out_keys.append(key)
            self.outs.append(jax.ShapeDtypeStruct((self.blocks,) + shape, dtype))
            self.out_specs.append(leading(shape))

    def temp(self, **forms):
        for key, (shape, dtype) in forms.items():
            self.temp_keys.append(key)
            self.temps.append(pltpu.VMEM(shape, dtype))

    def run(self, name, body):
        keys = self.keys + self.out_keys + self.temp_keys

        def kernel(*refs):
            r = SimpleNamespace()
            for key, ref in zip(keys, refs):
                if isinstance(key, tuple):
                    runs = r.__dict__.setdefault(key[0], {}).setdefault(key[1], {})
                    runs.setdefault(key[2], []).append(ref)
                elif key is not None:
                    setattr(r, key, ref)
            body(r)

        got = pl.pallas_call(
            kernel,
            grid=(self.blocks,),
            in_specs=self.specs,
            out_specs=self.out_specs,
            out_shape=self.outs,
            scratch_shapes=self.temps,
            cost_estimate=LIGHT,
            name=name,
        )(*self.arrays)
        return SimpleNamespace(**dict(zip(self.out_keys, got)))


LIGHT = pl.CostEstimate(flops=1, transcendentals=0, bytes_accessed=1)


def zeros(n):
    return lambda *g: (0,) * n


def leading(shape):
    rest = (0,) * len(shape)
    return pl.BlockSpec((None,) + shape, lambda b: (b,) + rest)


STEP = 32


def by_rows(rows, step, run):
    @pl.loop(0, rows // step)
    def _(i):
        run(pl.ds(pl.multiple_of(i * step, step), step))


def place_pieces(r, target, group, width):
    core = r.info[0]
    row = r.info[1]

    def put(runs):
        first = 0
        for parts in runs.values():
            size = width // len(parts)
            if len(parts) == 4:
                far = (1 - core) * 2
                at = [core * 2 + row, core * 2 + 1 - row, far + row, far + 1 - row]
            else:
                at = [core, 1 - core]
            cuts = [pl.ds(pl.multiple_of(a * size, size), size) for a in at]

            def move(here, start=first):
                for part, cut in zip(parts, cuts):
                    there = pl.ds(pl.multiple_of(start + here.start, STEP), STEP)
                    target[there, cut] = part[here, :]

            by_rows(parts[0].shape[0], STEP, move)
            first += parts[0].shape[0]

    if len(group) == 1:
        put(group[0])
    else:
        for block, runs in group.items():
            pl.when(pl.program_id(0) == block)(functools.partial(put, runs))


def downwards(r):
    across = r.document[...].astype(F32)
    rows = across.shape[1]
    return jnp.broadcast_to(across, (rows, rows)).T


def decays(r):
    down = downwards(r)
    rows = down.shape[0]
    n = lax.broadcasted_iota(jnp.int32, (rows, rows), 0)
    m = lax.broadcasted_iota(jnp.int32, (rows, rows), 1)
    allowed = (n >= m) & (down == r.document[...].astype(F32))
    spread = jnp.where(allowed, (n - m).astype(F32), 0.0)
    return lambda h: jnp.where(allowed, jnp.exp(spread * r.rates[h]), 0.0)


def half_columns(r, width):
    size = width // 2
    return [pl.ds(pl.multiple_of(a * size, size), size) for a in (r.info[0], 1 - r.info[0])]


def attend(own, name, source, document, shared, weights, heads, after=()):
    query_w, key_w, value_wt, gate_wt, out_w = weights
    blocks, unused, rows = document.shape
    width = query_w.shape[0]
    features = value_wt.shape[0]
    c = Call(blocks)
    c.scalars(info=shared.info, rates=shared.rates)
    c.whole(gain=shared.first_gain, bias=shared.first_bias, head_gain=shared.head_gain)
    c.cut(document=document)
    c.whole(qw=query_w, kw=key_w, vw=value_wt, gw=gate_wt)
    c.after(*after)
    if own:
        c.whole(x=source, ow=out_w)
        part = ((rows, width // 2), F32)
        c.result(near=part, away=part)
    else:
        c.pieces(x=source)
        c.temp(x_rows=((rows, width), F32))
    wide = ((rows, heads * KD), BF16)
    tall = ((features, rows), BF16)
    tall_f = ((features, rows), F32)
    c.results(
        normed=((rows, width), BF16),
        q=wide,
        k=wide,
        v=tall,
        s=((heads, rows, rows), BF16),
        g=tall_f,
        hat=tall_f,
        inv=((heads, 1, rows), F32),
        gated=tall,
    )

    def body(r):
        if own:
            x = r.x[...].astype(F32)
        else:
            place_pieces(r, r.x_rows, r.x, width)
            x = r.x_rows[...]
        hat, unused = standard(x, EPS, 1)
        normed = (hat * r.gain[...] + r.bias[...]).astype(BF16)
        r.normed[...] = normed
        r.q[...] = nn(normed, r.qw[...]).astype(BF16)
        r.k[...] = (nn(normed, r.kw[...]) * SCALE).astype(BF16)
        r.v[...] = nt(r.vw[...], normed).astype(BF16)
        r.g[...] = nt(r.gw[...], normed)
        decay = decays(r)
        for h in range(heads):
            kd = pl.ds(h * KD, KD)
            vd = pl.ds(h * VD, VD)
            score = (nt(r.q[:, kd], r.k[:, kd]) * decay(h)).astype(BF16)
            r.s[h] = score
            head_hat, head_inv = standard(nt(r.v[vd, :], score), HEAD_EPS, 0)
            r.hat[vd, :] = head_hat
            r.inv[h] = head_inv
            gates = r.g[vd, :]
            swish = gates * jax.nn.sigmoid(gates)
            r.gated[vd, :] = (swish * (head_hat * r.head_gain[vd, :])).astype(BF16)
        if own:
            for cut, out in zip(half_columns(r, width), (r.near, r.away)):
                out[...] = tn(r.gated[...], r.ow[:, cut])

    return c.run(name, body)


def feed(own, name, middle, top, shared, weights, after=()):
    inner_wt, linear_wt, down_w = weights
    features, width = inner_wt.shape
    blocks, rows = len(middle), shared.rows
    c = Call(blocks)
    c.scalars(info=shared.info)
    c.whole(gain=shared.second_gain, bias=shared.second_bias)
    c.pieces(m=middle)
    c.whole(iw=inner_wt, lw=linear_wt, dw=down_w)
    c.after(*after)
    c.temp(m_rows=((rows, width), F32))
    if own:
        c.whole(c=top)
        part = ((rows, width // 2), F32)
        c.result(two_near=part, two_away=part, ff_near=part, ff_away=part)
    else:
        c.pieces(c=top)
        c.temp(c_rows=((rows, width), F32))
    flat = ((rows, width), BF16)
    tall = ((features, rows), BF16)
    c.results(normed=flat, top=flat, hidden=tall, gi=tall, gl=tall)

    def body(r):
        place_pieces(r, r.m_rows, r.m, width)
        hat, unused = standard(r.m_rows[...], EPS, 1)
        r.normed[...] = (hat * r.gain[...] + r.bias[...]).astype(BF16)
        if own:
            r.top[...] = r.c[...]
        else:
            place_pieces(r, r.c_rows, r.c, width)
            r.top[...] = r.c_rows[...].astype(BF16)
        def units(cut):
            inner = nt(r.iw[cut, :], r.normed[...])
            linear = nt(r.lw[cut, :], r.normed[...])
            upstream = nt(r.dw[cut, :], r.top[...])
            cumulative = 0.5 * (1.0 + lax.erf(inner * 0.7071067811865476))
            gelu = inner * cumulative
            slope = cumulative + inner * jnp.exp(-0.5 * inner * inner) * 0.3989422804014327
            r.hidden[cut, :] = (gelu * linear).astype(BF16)
            r.gi[cut, :] = (upstream * linear * slope).astype(BF16)
            r.gl[cut, :] = (upstream * gelu).astype(BF16)

        by_rows(features, VD, units)
        if own:
            cuts = half_columns(r, width)
            for cut, out in zip(cuts, (r.two_near, r.two_away)):
                out[...] = tn(r.gi[...], r.iw[:, cut]) + tn(r.gl[...], r.lw[:, cut])
            for cut, out in zip(cuts, (r.ff_near, r.ff_away)):
                out[...] = tn(r.hidden[...], r.dw[:, cut])

    return c.run(name, body)


def add_sums(r, upstream, hat):
    @pl.when(pl.program_id(0) == 0)
    def _():
        r.gain_sum[...] = jnp.zeros(r.gain_sum.shape, F32)
        r.bias_sum[...] = jnp.zeros(r.bias_sum.shape, F32)

    r.gain_sum[...] += jnp.sum(upstream * hat, 0, keepdims=True)
    r.bias_sum[...] += jnp.sum(upstream, 0, keepdims=True)


def middle_back(middle, upstream, top, shared, after=()):
    rows, width = top.shape
    c = Call(4, rows)
    c.scalars(info=shared.info)
    c.whole(gain=shared.second_gain, top=top)
    c.pieces(m=middle, u=upstream)
    c.after(*after)
    flat = ((rows, width), F32)
    line = ((1, width), F32)
    part = ((rows // 4, width), F32)
    c.temp(m_rows=part, u_rows=part)
    c.result(grad=flat, half=((rows, width // 2), F32), gain_sum=line, bias_sum=line)
    c.result(quarter=((rows, width // 4), F32))

    def body(r):
        place_pieces(r, r.m_rows, r.m, width)
        place_pieces(r, r.u_rows, r.u, width)
        hat, inverse = standard(r.m_rows[...], EPS, 1)
        upstream = r.u_rows[...]
        add_sums(r, upstream, hat)
        r.grad[...] = r.top[...].astype(F32) + norm_back(
            upstream, hat, inverse, r.gain[...], 1
        )
        r.half[...] = r.grad[:, half_columns(r, width)[0]]
        n = width // 4
        at = (r.info[0] * 2 + r.info[1]) * n
        r.quarter[...] = r.grad[:, pl.ds(pl.multiple_of(at, n), n)]

    return c.run("middle_back", body)


def back(own, name, grad, state, document, shared, weights, heads, after=()):
    query_w, key_w, value_wt, gate_wt, out_w = weights
    width = query_w.shape[0]
    features = value_wt.shape[0]
    blocks, unused, rows = document.shape
    c = Call(blocks)
    c.scalars(info=shared.info, rates=shared.rates)
    c.whole(head_gain=shared.head_gain)
    c.cut(document=document)
    c.cut(q=state.q, k=state.k, v=state.v, s=state.s, g=state.g, hat=state.hat, inv=state.inv)
    c.whole(ow=out_w)
    c.after(*after)
    if own:
        c.whole(m=grad, qw=query_w, kw=key_w, vw=value_wt, gw=gate_wt)
        part = ((rows, width // 2), F32)
        c.result(near=part, away=part, head_sum=((features, 1), F32))
    else:
        c.pieces(m=grad)
        c.temp(m_rows=((rows, width), F32))
    wide = ((rows, heads * KD), BF16)
    tall = ((features, rows), BF16)
    c.results(gm=((rows, width), BF16), gq=wide, gk=wide, gv=tall, gg=tall)

    def body(r):
        if own:
            r.gm[...] = r.m[...].astype(BF16)
        else:
            place_pieces(r, r.m_rows, r.m, width)
            r.gm[...] = r.m_rows[...].astype(BF16)
        decay = decays(r)
        @pl.loop(0, heads)
        def _(h):
            kd = pl.ds(pl.multiple_of(h * KD, KD), KD)
            vd = pl.ds(pl.multiple_of(h * VD, VD), VD)
            grad_gated = nt(r.ow[vd, :], r.gm[...])
            gates = r.g[vd, :]
            head_hat = r.hat[vd, :]
            gain = r.head_gain[vd, :]
            sigma = jax.nn.sigmoid(gates)
            r.gg[vd, :] = (
                grad_gated * (head_hat * gain) * sigma * (1.0 + gates * (1.0 - sigma))
            ).astype(BF16)
            grad_normed = grad_gated * (gates * sigma)
            if own:
                r.head_sum[vd, :] = jnp.sum(grad_normed * head_hat, 1, keepdims=True)
            mixed = norm_back(grad_normed, head_hat, r.inv[h], gain, 0).astype(BF16)
            masked = (tn(mixed, r.v[vd, :]) * decay(h)).astype(BF16)
            r.gv[vd, :] = nn(mixed, r.s[h]).astype(BF16)
            r.gq[:, kd] = nn(masked, r.k[:, kd]).astype(BF16)
            r.gk[:, kd] = (tn(masked, r.q[:, kd]) * SCALE).astype(BF16)
        if own:
            for cut, out in zip(half_columns(r, width), (r.near, r.away)):
                out[...] = (
                    nt(r.gq[...], r.qw[cut, :])
                    + nt(r.gk[...], r.kw[cut, :])
                    + tn(r.gv[...], r.vw[:, cut])
                    + tn(r.gg[...], r.gw[:, cut])
                )

    return c.run(name, body)


def weigh(name, terms, which, after=()):
    arrays, specs, outs, out_specs = [], [], [], []
    ends = []
    for array in terms[0][0]:
        ends.append(array.shape[0] + (ends[-1] if ends else 0))

    def at(i, b):
        count = terms[0][0][i].shape[0]
        return jnp.clip(b - (ends[i] - count), 0, count - 1) if count > 1 else 0

    for lefts, rights, turned, size in terms:
        for i, left in enumerate(lefts):
            arrays.append(left)
            specs.append(
                pl.BlockSpec((None, left.shape[1], size), lambda b, w, i=i: (at(i, b), 0, w[0]))
            )
        for i, right in enumerate(rights):
            arrays.append(right)
            specs.append(
                pl.BlockSpec((None,) + right.shape[1:], lambda b, w, i=i: (at(i, b), 0, 0))
            )
        shape = (size, right.shape[2]) if turned else (right.shape[1], size)
        outs.append(jax.ShapeDtypeStruct(shape, F32))
        out_specs.append(pl.BlockSpec(shape, lambda b, w: (0, 0)))
    for array in after:
        arrays.append(array)
        specs.append(pl.BlockSpec(memory_space=pl.ANY))
    n = len(ends)

    def kernel(w, *refs):
        results = refs[len(arrays) :]
        b = pl.program_id(0)

        def pick(some):
            value = some[-1][...]
            for end, ref in zip(ends[-2::-1], some[-2::-1]):
                value = lax.select(b < end, ref[...], value)
            return value

        for i, result in enumerate(results):
            left = pick(refs[2 * n * i : 2 * n * i + n])
            right = pick(refs[2 * n * i + n : 2 * n * i + 2 * n])
            got = tn(left, right) if terms[i][2] else nn(right, left)
            result[...] = lax.select(b > 0, result[...], jnp.zeros_like(got)) + got

    return pl.pallas_call(
        kernel,
        grid_spec=pltpu.PrefetchScalarGridSpec(
            num_scalar_prefetch=1, grid=(ends[-1],), in_specs=specs, out_specs=out_specs
        ),
        out_shape=outs,
        cost_estimate=LIGHT,
        name=name,
    )(which, *arrays)


def joined(pieces, info, width, after=()):
    rows = pieces[0].shape[0]
    c = Call(4, rows)
    c.scalars(info=info)
    c.pieces(y=[[pieces]])
    c.after(*after)
    c.result(out=((rows, width), F32))
    return c.run("joined", lambda r: place_pieces(r, r.out, r.y, width)).out


def input_gradient(pieces, inputs, middle, info, gain, after=()):
    rows, width = inputs.shape
    c = Call(4, rows)
    c.scalars(info=info)
    c.whole(gain=gain, x=inputs, middle=middle)
    c.pieces(u=[[pieces]])
    c.after(*after)
    line = ((1, width), F32)
    c.result(out=((rows, width), F32), gain_sum=line, bias_sum=line)
    c.temp(u_rows=((rows // 4, width), F32))

    def body(r):
        place_pieces(r, r.u_rows, r.u, width)
        hat, inverse = standard(r.x[...].astype(F32), EPS, 1)
        upstream = r.u_rows[...]
        add_sums(r, upstream, hat)
        r.out[...] = r.middle[...] + norm_back(upstream, hat, inverse, r.gain[...], 1)

    return c.run("finish", body)


def make_body(dp, tp):
    hi_count = dp // BITS

    def permute(x, target):
        pairs = []
        for d in range(dp):
            for t in range(tp):
                to_d, to_t = target(d, t)
                pairs.append((d * tp + t, to_d * tp + to_t))
        return lax.ppermute(x, AXES, pairs)

    swap_core = lambda x: permute(x, lambda d, t: (d, t ^ 1))
    swap_row = lambda x: permute(x, lambda d, t: (d, t ^ 2))
    swap_dp = lambda x, bit: permute(x, lambda d, t: (d ^ bit, t))

    gate = lambda x, earlier: lax.optimization_barrier((x,) + tuple(earlier))[0] if earlier else x

    class Stages:
        def __init__(self):
            self.before, self.now, self.sends = [], [], 0
            self.spare, self.fresh = [], []

        def send(self, swap, x, free=False):
            got = swap(x if free else gate(x, self.before))
            self.now.append(got)
            self.sends += 1
            return got

        def ran(self, *arrays):
            self.now += arrays

        def later(self, x):
            slot = [x, None]
            self.fresh.append(slot)
            return slot

        def end(self, limit=5):
            while self.spare and self.sends < limit:
                slot = self.spare.pop(0)
                slot[1] = self.send(swap_core, slot[0])
            self.spare, self.fresh = self.spare + self.fresh, []
            self.before, self.now, self.sends = self.now, [], 0

    def body(
        inputs,
        document,
        query_weight,
        key_weight,
        value_weight,
        gate_weight,
        out_weight,
        inner_weight,
        linear_weight,
        down_weight,
        first_gain,
        first_bias,
        head_gain,
        second_gain,
        second_bias,
        cotangent,
    ):
        rows, width = inputs.shape
        share = width // dp
        heads = query_weight.shape[1] // KD
        d = lax.axis_index("dp")
        t = lax.axis_index("tensor")
        core = t % 2
        row = t // 2
        info = jnp.stack([core, row]).astype(jnp.int32)
        numbers = (t * heads + jnp.arange(heads)).astype(F32)
        shared = SimpleNamespace(
            info=info,
            rows=rows,
            rates=jnp.log1p(-jnp.exp2(-5.0 - numbers)),
            first_gain=first_gain[None],
            first_bias=first_bias[None],
            second_gain=second_gain[None],
            second_bias=second_bias[None],
            head_gain=head_gain[:, None],
        )
        attention = (query_weight, key_weight, value_weight.T, gate_weight.T, out_weight)
        hidden_layer = (inner_weight.T, linear_weight.T, down_weight)

        low = d % BITS

        def share_of(x, place):
            cuts = [
                lax.dynamic_slice_in_dim(x, (hi * BITS + place) * share, share, x.ndim - 1)
                for hi in range(hi_count)
            ]
            return jnp.concatenate(cuts, x.ndim - 1)

        def over_hi(x, axis):
            hi = d // BITS
            cut = lambda k: lax.dynamic_slice_in_dim(x, (hi ^ k) * share, share, axis)
            total = cut(0)
            for k in range(1, hi_count):
                total = total + swap_dp(cut(k), k * BITS)
            return total

        def product(name, terms, place, after=()):
            ready = []
            for lefts, rights, turned in terms:
                if hi_count > 1:
                    lefts = [share_of(left, place) for left in lefts]
                ready.append((lefts, rights, turned, hi_count * share))
            index = place if hi_count == 1 else place * 0
            return weigh(name, ready, index.reshape(1).astype(jnp.int32), after)

        def finished(mine, arrived, axis=1):
            total = gate(mine, at.before) + arrived
            return over_hi(total, axis) if hi_count > 1 else total

        def term(lefts, rights, turned=False):
            return (lefts, rights, turned)

        side = lambda x: swap_dp(x, SIDE)
        following = lambda x: swap_dp(x, NEXT)
        far = lambda x: swap_dp(x, FAR)
        stack = lambda *parts: jnp.concatenate(parts, 0)

        def half(array):
            return lax.dynamic_slice_in_dim(array, core * (width // 2), width // 2, 1).astype(F32)

        def quarter(halved):
            return lax.dynamic_slice_in_dim(halved, row * (width // 4), width // 4, 1)

        def pairs(*slots):
            return [[slot[0], slot[1]] for slot in slots]

        def quads(one, two):
            return [[one[0], two[0], one[1], two[1]]]

        own_doc = document[None, None]
        live = (document < DOCS_DEV)[:, None]
        top = jnp.where(live, cotangent, jnp.zeros((), BF16))
        top_quarter = quarter(half(top))
        input_half = half(inputs)
        k = rows // 4
        at = Stages()

        doc_side = at.send(side, document)
        doc_far = at.send(far, document)
        x_side = [at.later(at.send(side, input_half[: 2 * k]))]
        t_next = at.later(at.send(following, top_quarter))
        x_far = [None, at.later(at.send(far, input_half[2 * k : 3 * k]))]
        own = attend(True, "attend_own", inputs, own_doc, shared, attention, heads)
        at.ran(own.near)
        at.end(0)

        branch = own.near + at.send(swap_core, own.away)
        at.end(2)

        branch_row = at.send(swap_row, branch)
        doc_both = at.send(side, doc_far)
        x_side.append(at.later(at.send(side, input_half[2 * k :])))
        x_far[0] = at.later(at.send(far, input_half[: 2 * k]))
        at.end()
        middle = input_half + (branch + branch_row)

        middle_core = at.send(swap_core, middle)
        at.end(3)

        x_far.append(at.later(at.send(far, input_half[3 * k :])))
        x_both = [at.later(at.send(side, x_far[0][0]))]
        t_next_row = at.later(at.send(swap_row, t_next[0]))
        middle_own = [[[middle, middle_core]]]
        fed = feed(True, "feed_own", middle_own, top, shared, hidden_layer, at.before)
        at.ran(fed.two_near)
        at.end()

        two = fed.two_near + at.send(swap_core, fed.two_away)
        at.end(2)

        two_row = at.send(swap_row, two)
        m_next = at.later(at.send(following, quarter(middle)))
        m_far = at.later(at.send(far, quarter(middle)))
        x_both.append(at.later(at.send(side, stack(x_far[1][0], x_far[2][0]))))
        ff = fed.ff_near + at.send(swap_core, fed.ff_away)
        at.ran(ff)
        at.end()
        two = two + two_row

        two_core = at.send(swap_core, two)
        at.end(4)

        grad = middle_back(middle_own, [[[two, two_core]]], top, shared, at.before)
        at.ran(grad.grad)
        at.end(9)

        g_side = at.send(side, grad.half)
        g_far = at.send(far, grad.quarter)
        m_next_row = at.send(swap_row, m_next[0])
        m_far_row = at.send(swap_row, m_far[0])
        m_next_row, g_side, g_far, m_far_row = map(
            at.later, (m_next_row, g_side, g_far, m_far_row)
        )
        other_doc = jnp.stack([doc_side, doc_far, doc_both])[:, None]
        others = attend(
            False,
            "attend",
            [pairs(*x_side), pairs(*x_far), pairs(*x_both)],
            other_doc,
            shared,
            attention,
            heads,
            at.before,
        )
        at.ran(others.q)
        at.end()

        g_both = at.later(at.send(side, g_far[0]))
        g_far_row = at.later(at.send(swap_row, g_far[0]))
        m_both = at.later(at.send(following, m_far[0]))
        t_far = at.send(far, top_quarter[: 2 * k])
        backed = back(
            True, "back_own", grad.grad, own, own_doc, shared, attention, heads, at.before
        )
        at.ran(backed.near)
        at.end()

        g_both_row = at.send(swap_row, g_both[0])
        t_far = stack(t_far, at.send(far, top_quarter[2 * k :]))
        one = backed.near + at.send(swap_core, backed.away)
        first_fed = feed(
            False,
            "feed_next",
            [quads(m_next, m_next_row)],
            [quads(t_next, t_next_row)],
            shared,
            hidden_layer,
            at.before,
        )
        at.ran(first_fed.gi)
        at.end()
        t_far = at.later(t_far)

        g_both_row = [g_both_row, at.send(swap_core, g_both_row)]
        at.end(5)

        t_both = at.later(at.send(following, t_far[0]))
        m_both_row = at.later(at.send(swap_row, m_both[0]))
        t_far_row = at.later(at.send(swap_row, t_far[0]))
        other_backed = back(
            False,
            "back",
            [pairs(g_side), quads(g_far, g_far_row), quads(g_both, g_both_row)],
            others,
            other_doc,
            shared,
            attention,
            heads,
            at.before,
        )
        first_normed = [own.normed, others.normed]
        value_terms = [
            term([backed.gm, other_backed.gm], [own.gated, others.gated]),
            term(first_normed, [backed.gg, other_backed.gg]),
            term(first_normed, [backed.gv, other_backed.gv]),
        ]
        key_terms = [
            term(first_normed, [backed.gq, other_backed.gq], True),
            term(first_normed, [backed.gk, other_backed.gk], True),
        ]
        key_sent = product("key_partial", key_terms, low ^ NEXT, at.before)
        at.ran(other_backed.gq, key_sent[0])
        at.end()

        t_both_row = at.send(swap_row, t_both[0])
        key_came = [at.send(following, key_sent[0])]
        value_sent = product("value_partial", value_terms, low ^ NEXT, at.before)
        at.ran(value_sent[0], one)
        at.end(6)

        t_both_row = [t_both_row, at.send(swap_core, t_both_row)]
        at.end(4)

        value_came = [at.send(following, value_sent[0])]
        one_row = at.send(swap_row, one)
        other_fed = feed(
            False,
            "feed",
            [quads(m_far, m_far_row), quads(m_both, m_both_row)],
            [quads(t_far, t_far_row), quads(t_both, t_both_row)],
            shared,
            hidden_layer,
            at.before,
        )
        feds = [fed, first_fed, other_fed]
        second_normed = [f.normed for f in feds]
        mlp_terms = [
            term([f.top for f in feds], [f.hidden for f in feds]),
            term(second_normed, [f.gi for f in feds]),
            term(second_normed, [f.gl for f in feds]),
        ]
        mlp_sent = product("mlp_partial", mlp_terms, low ^ SIDE, at.before)
        at.ran(mlp_sent[0])
        at.end()
        one = one + one_row

        value_came.append(at.send(following, value_sent[1]))
        mlp_came = [at.send(side, mlp_sent[0])]
        one_core = at.send(swap_core, one)
        ff_row = at.send(swap_row, ff)
        value_mine = product("value_mine", value_terms, low, at.before)
        key_mine = product("key_mine", key_terms, low, at.before)
        mlp_mine = product("mlp_mine", mlp_terms, low, at.before)
        at.ran(value_mine[0], key_mine[0], mlp_mine[0])
        at.end()
        ff = middle + (ff + ff_row)

        value_came.append(at.send(following, value_sent[2]))
        mlp_came.append(at.send(side, mlp_sent[1]))
        ff_core = at.send(swap_core, ff)
        finish = input_gradient(
            [one, one_core],
            inputs,
            grad.grad,
            info,
            shared.first_gain,
            at.before,
        )
        sums = jnp.concatenate(
            [
                grad.gain_sum[0],
                grad.bias_sum[0],
                finish.gain_sum[0],
                finish.bias_sum[0],
                backed.head_sum[:, 0],
            ]
        )
        sums = sums + at.send(side, sums, free=True)
        at.ran(finish.out)
        at.end()

        mlp_came.append(at.send(side, mlp_sent[2]))
        key_came.append(at.send(following, key_sent[1]))
        outputs = joined([ff, ff_core], info, width, at.before)
        grad_down, grad_inner, grad_linear = map(finished, mlp_mine, mlp_came)
        grad_out, grad_gate, grad_value = map(finished, value_mine, value_came)
        grad_query, grad_key = [finished(a, b, 0) for a, b in zip(key_mine, key_came)]

        ready = (key_came[1], outputs, grad_down, grad_inner, grad_out, grad_gate, grad_value)
        sums_next, sums_far, sums_both = [
            swap_dp(gate(sums, ready), bit) for bit in (NEXT, FAR, NEXT | FAR)
        ]
        sums = (sums + sums_next) + (sums_far + sums_both)
        bit = BITS
        while bit < dp:
            sums = sums + swap_dp(sums, bit)
            bit *= 2
        vector = lambda i: sums[i * width : (i + 1) * width]
        return (
            outputs,
            finish.out,
            grad_query,
            grad_key,
            grad_value.T,
            grad_gate.T,
            grad_out,
            grad_inner.T,
            grad_linear.T,
            grad_down,
            vector(2),
            vector(3),
            sums[4 * width :],
            vector(0),
            vector(1),
        )

    return body


def solution(mesh):
    in_specs = (
        P("dp", None),
        P("dp"),
        P(None, "tensor"),
        P(None, "tensor"),
        P(None, "tensor"),
        P(None, "tensor"),
        P("tensor", None),
        P(None, "tensor"),
        P(None, "tensor"),
        P("tensor", None),
        P(),
        P(),
        P("tensor"),
        P(),
        P(),
        P("dp", None),
    )
    out_specs = (
        P("dp", None),
        P("dp", None),
        P("dp", "tensor"),
        P("dp", "tensor"),
        P("dp", "tensor"),
        P("dp", "tensor"),
        P("tensor", "dp"),
        P("dp", "tensor"),
        P("dp", "tensor"),
        P("tensor", "dp"),
        P(),
        P(),
        P("tensor"),
        P(),
        P(),
    )
    body = make_body(mesh.shape["dp"], mesh.shape["tensor"])
    return jax.shard_map(body, mesh=mesh, in_specs=in_specs, out_specs=out_specs, check_vma=False)
```
